512 devices in a mesh: dp: 8 (over y), expert: 64 (over z, x, core).
Axes of the slice: x: 4, y: 8, z: 8, core: 2. Of those that a mesh axis runs over, the one named last changes fastest.
Arguments:
- tokens: bfloat16 [4096, 4096], P('expert', 'dp'), may hold values from -6 to 6
- expert_ids: int32 [4096, 8], P('expert'), may hold values from 0 to 63, all different within a row; in each aligned block of 64 rows (0 to 63, 64 to 127, ...) at most 16 rows name the same one
- gate_weights: float32 [4096, 8], P('expert'), may hold values from 0.05 to 1
- gate_proj: bfloat16 [64, 4096, 1536], P('expert', 'dp'), may hold values from -0.09375 to 0.09375
- up_proj: bfloat16 [64, 4096, 1536], P('expert', 'dp'), may hold values from -0.09375 to 0.09375
- down_proj: bfloat16 [64, 1536, 4096], P('expert', None, 'dp'), may hold values from -0.15625 to 0.15625
Outputs:
- combined: bfloat16 [4096, 4096], P('expert', 'dp')
The draws below stay inside these ranges and needn't reach their ends.
Inputs may be any that keep to these rules, and one draw needn't show every extreme that they name: `expert_ids`: each row names 8 different experts. Among the 64 rows of one device (one aligned block), no expert is named by more than 16 rows, and in every draw some expert is named by exactly 16 rows of some block.
All inputs are finite; a program needn't handle non-finite values.
Results may differ from the reference program's by a relative error of at most 0.029.
Values may be sent and summed in bfloat16 or wider, within the bound.
A program may use at most 64 MiB of HBM per device.

```python
import math
import jax
import jax.numpy as jnp
import numpy as np
from jax import lax

D = 4096
FF = 1536
TOPK = 8
TOK_DEV = 64
EXPERTS = 64
CAP = 16
TOKENS = 4096
N_DP = 8
N_EXPERT = 64


def block_levels(stream_key, shape, shards, low, top_value):
    def one(dim, shards_of):
        heights = jax.random.uniform(jax.random.fold_in(jax.random.fold_in(stream_key, 6), dim), (shards_of,), jnp.float32, low / len(shards), top_value / len(shards))
        return jnp.repeat(jnp.exp(heights), shape[dim] // shards_of).reshape((-1,) + (1,) * (len(shape) - dim - 1))

    level = one(*shards[0])
    for cut in shards[1:]:
        level = level * one(*cut)
    return level


def assign_block(stream_key, own, number, rows, amount, top, reach, skew):
    order = jax.random.permutation(stream_key, amount)
    crowded, ordinary = shares(amount, rows * top, reach, skew, True), shares(amount, rows * top, reach, skew, False)
    places = jnp.arange(amount)

    def named(tallies, offset_by):
        used = int((tallies > 0).sum())
        fixed = max(1, used // 4)
        moved = fixed + (places - fixed + offset_by * (used - fixed)) % max(1, amount - fixed)
        return jnp.zeros((amount,), jnp.int32).at[order[jnp.where(places < fixed, places, moved)]].set(jnp.asarray(tallies, jnp.int32))

    tallies = jnp.where(number % 4 == 0, named(crowded, number // 4), named(ordinary, number - number // 4 - 1))
    mixed = jax.random.permutation(jax.random.fold_in(own, 3), amount)
    source_of, taker = mixed[0:amount // 2 * 2:2], mixed[1:amount // 2 * 2:2]
    room = jnp.minimum(tallies[source_of] - 1, reach - tallies[taker]) // 2
    room = jnp.where((source_of == order[0]) | (taker == order[0]) | (tallies[taker] == 0), 0, jnp.maximum(room, 0))
    moved = jax.random.randint(jax.random.fold_in(own, 4), (amount // 2,), 0, 1 << 20) % (room + 1)
    tallies = tallies.at[source_of].add(-moved).at[taker].add(moved)
    members = jnp.searchsorted(jnp.cumsum(tallies), jnp.arange(rows * top), side="right").astype(jnp.int32)
    table = members.reshape(top, rows).T
    table = table[jax.random.permutation(jax.random.fold_in(own, 1), rows)]
    offset_by = jax.random.randint(jax.random.fold_in(own, 2), (rows, 1), 0, top)
    return jnp.take_along_axis(table, (jnp.arange(top)[None, :] + offset_by) % top, axis=1)


def shares(amount, total, reach, slope, full):
    weights = [(1 << 20) // math.isqrt(standing ** slope) + 1 for standing in range(1, amount + 1)]
    largest = reach if full else min(reach, max(-(-total // amount), total * weights[0] // sum(weights)))
    least = 1 if total - largest >= amount - 1 else 0
    holding, spare = [largest] + [least] * (amount - 1), total - largest - least * (amount - 1)
    while spare > 0:
        candidates = [i for i in range(1, amount) if holding[i] < largest] or [i for i in range(1, amount) if holding[i] < reach]
        pool, left = sum([weights[i] for i in candidates]), spare
        for i in candidates:
            addition = min(reach - holding[i], max(1, left * weights[i] // pool), spare)
            holding[i] = holding[i] + addition
            spare = spare - addition
    return np.array(holding)


def noise(stream_key, extent, scale, reach, split=(), held_as=jnp.bfloat16):
    result = jax.random.normal(stream_key, extent, jnp.float32) * scale
    if len(split) > 0:
        result = block_levels(stream_key, extent, split, -0.22, 0.18) * result
    return jnp.clip(result, min=-reach, max=reach).astype(held_as)


def setup_inputs(seed: int = 0) -> dict:
    keys = jax.random.split(jax.random.key(seed), 7)
    tokens = noise(keys[0], (TOKENS, D), 1.0, 6.0, ((0, 64), (1, 8)))
    expert_ids_keys = jax.random.split(jax.random.fold_in(keys[1], 1), TOKENS // TOK_DEV)
    expert_ids_turns = jax.random.permutation(jax.random.fold_in(keys[1], 3), TOKENS // TOK_DEV)
    expert_ids = jax.vmap(lambda own, number: assign_block(jax.random.fold_in(keys[1], 2), own, number, TOK_DEV, EXPERTS, TOPK, CAP, 2))(expert_ids_keys, expert_ids_turns).reshape((TOKENS, TOPK))
    gate_weights = jnp.clip(jnp.exp(math.log(1.0) - 2.9957323 * jax.random.uniform(keys[2], (TOKENS, TOPK), jnp.float32) ** block_levels(keys[2], (TOKENS, TOPK), ((0, 64),), -0.2, 0.2)), 0.05, 1.0)
    gate_proj = noise(keys[3], (EXPERTS, D, FF), D ** -0.5, 0.09375, ((0, 64), (1, 8)))
    up_proj = noise(keys[4], (EXPERTS, D, FF), D ** -0.5, 0.09375, ((0, 64), (1, 8)))
    down_proj = noise(keys[5], (EXPERTS, FF, D), FF ** -0.5, 0.15625, ((0, 64), (2, 8)))
    return {"tokens": tokens, "expert_ids": expert_ids, "gate_weights": gate_weights, "gate_proj": gate_proj, "up_proj": up_proj, "down_proj": down_proj}


def block_places(block_ids, expert_count, capacity):
    tok_count, top_count = block_ids.shape
    flat_ids = block_ids.reshape(tok_count * top_count)
    matches = (flat_ids[:, None] == jnp.arange(expert_count, dtype=jnp.int32)[None, :]).astype(jnp.int32)
    earlier = jnp.cumsum(matches, axis=0) - matches
    slot_index = jnp.sum(earlier * matches, axis=1)
    return (flat_ids * capacity + slot_index).reshape(tok_count, top_count)


def reference(tokens, expert_ids, gate_weights, gate_proj, up_proj, down_proj):
    shard_width = D // N_DP
    id_blocks = expert_ids.reshape(N_EXPERT, TOK_DEV, TOPK)

    def place_one(block_ids):
        return block_places(block_ids, EXPERTS, CAP)

    places = jax.vmap(place_one)(id_blocks)
    source_tokens = tokens.astype(jnp.float32).reshape(N_EXPERT, TOK_DEV, D)
    route_weights = gate_weights.reshape(N_EXPERT, TOK_DEV, TOPK)
    slot_range = jnp.arange(CAP, dtype=jnp.int32)

    def one_expert(totals, expert_index):
        targets = expert_index * CAP + slot_range
        matches = places[:, :, :, None] == targets[None, None, None, :]
        chosen = jnp.any(matches, axis=2).astype(jnp.float32)
        weighting = jnp.sum(jnp.where(matches, route_weights[:, :, :, None], 0.0), axis=2)
        row_block = jnp.einsum('stc,std->scd', chosen, source_tokens, precision=lax.Precision.HIGHEST)
        pieces = row_block.reshape(N_EXPERT * CAP, N_DP, shard_width)
        gate_w = gate_proj[expert_index].astype(jnp.float32).reshape(N_DP, shard_width, FF)
        up_w = up_proj[expert_index].astype(jnp.float32).reshape(N_DP, shard_width, FF)
        gate_part = jnp.einsum('rjd,jdf->rjf', pieces, gate_w, precision=lax.Precision.HIGHEST)
        up_part = jnp.einsum('rjd,jdf->rjf', pieces, up_w, precision=lax.Precision.HIGHEST)
        gate_part = lax.optimization_barrier(gate_part.astype(jnp.bfloat16))
        up_part = lax.optimization_barrier(up_part.astype(jnp.bfloat16))
        gate_sum = jnp.sum(gate_part.astype(jnp.float32), axis=1)
        up_sum = jnp.sum(up_part.astype(jnp.float32), axis=1)
        hidden = (jax.nn.silu(gate_sum) * up_sum).astype(jnp.bfloat16)
        expert_out = jnp.dot(hidden, down_proj[expert_index], preferred_element_type=jnp.float32).astype(jnp.bfloat16)
        out_block = expert_out.astype(jnp.float32).reshape(N_EXPERT, CAP, D)
        added = jnp.einsum('stc,scd->std', weighting, out_block, precision=lax.Precision.HIGHEST)
        return totals + added, None

    start = jnp.zeros((N_EXPERT, TOK_DEV, D), jnp.float32)
    totals, unused = lax.scan(one_expert, start, jnp.arange(EXPERTS, dtype=jnp.int32))
    return totals.reshape(TOKENS, D).astype(jnp.bfloat16)
```

```python
import functools

import jax
import jax.numpy as jnp
from jax import lax
from jax.experimental import pallas as pl
from jax.experimental.pallas import tpu as pltpu
from jax.sharding import PartitionSpec as P

MESH = pl.DeviceIdType.MESH
F32 = jnp.float32
BF16 = jnp.bfloat16


def quotient(a, b):
    return a // b if isinstance(a, int) else lax.div(a, jnp.int32(b))


def residue(a, b):
    return a % b if isinstance(a, int) else lax.rem(a, jnp.int32(b))


def iota(shape, dim):
    return lax.broadcasted_iota(jnp.int32, shape, dim)


def layer(
    n, per, ids_hbm, gw_hbm, tok_hbm, gate_hbm, up_hbm, down_hbm, out_ref,
    ids_ref, gw_ref, tok_ref, w_buf, d_buf, code_ref, mix_ref, packed, rows, rs_out, rs_in, hid, outs, ret,
    load_sem, pack_send, pack_recv, rs_send, rs_recv, ag_send, ag_recv, ret_send, ret_recv,
):
    y = lax.axis_index("dp")
    me = lax.axis_index("expert")
    z, r = quotient(me, per), residue(me, per)
    x, c = quotient(r, 2), residue(r, 2)
    n_x, half, mid = per // 2, per // 2, n // 2
    experts = n * per
    top, toks = ids_ref.shape
    width = tok_ref.shape[1]
    cap = packed.shape[2]
    m_rows = half * cap
    ff = w_buf.shape[2]
    tile = min(ff, 512)
    sub_rows = m_rows // 2
    ahead, behind = residue(y + 1, n), residue(y + n - 1, n)
    steps = n - 1

    small = [
        pltpu.make_async_copy(ids_hbm, ids_ref, load_sem.at[3]),
        pltpu.make_async_copy(gw_hbm, gw_ref, load_sem.at[4]),
        pltpu.make_async_copy(tok_hbm, tok_ref, load_sem.at[5]),
    ]
    loads = [
        pltpu.make_async_copy(gate_hbm, w_buf.at[0], load_sem.at[0]),
        pltpu.make_async_copy(up_hbm, w_buf.at[1], load_sem.at[1]),
        pltpu.make_async_copy(down_hbm, d_buf, load_sem.at[2]),
    ]
    for load in small + loads:
        load.start()
    barrier = pltpu.get_barrier_semaphore()

    def greet(i, carry):
        pl.semaphore_signal(
            barrier, inc=1, device_id={"expert": residue(me + i, experts)}, device_id_type=MESH
        )
        return carry

    lax.fori_loop(1, experts, greet, 0)
    for to in (ahead, behind):
        pl.semaphore_signal(barrier, inc=1, device_id={"dp": to}, device_id_type=MESH)
    for load in small:
        load.wait()

    expert_of = iota((experts, toks), 0)
    named = jnp.zeros((experts, toks), F32)
    picked = jnp.zeros((experts, toks), F32)
    for k in range(top):
        same = ids_ref[k : k + 1, :] == expert_of
        named = named + jnp.where(same, 1.0, 0.0)
        picked = picked + jnp.where(same, gw_ref[k : k + 1, :], 0.0)
    before = jnp.where(iota((toks, toks), 0) < iota((toks, toks), 1), 1.0, 0.0).astype(BF16)
    earlier = jnp.dot(named.astype(BF16), before, preferred_element_type=F32)
    code = jnp.where(named > 0.0, earlier, -1.0)
    code_ref[...] = code

    pl.semaphore_wait(barrier, experts - 1 + 2)

    def at_distance(i):
        k = mid - quotient(i + 1, 2)
        odd = residue(i, 2)
        return residue(y + odd * k + (1 - odd) * (n - k), n)

    def send_rows(p, h):
        to_z = residue(z + n - p, n)
        for j in range(half):
            dx, dc = divmod(h * half + j, 2)
            to_r = residue(x + n_x - dx, n_x) * 2 + residue(c + dc, 2)
            src, dst = packed.at[to_z, to_r], rows.at[p * 2 + h, j]
            sem = pack_recv.at[p * 2 + h]

            def remote():
                pltpu.make_async_remote_copy(
                    src_ref=src, dst_ref=dst, send_sem=pack_send, recv_sem=sem,
                    device_id={"expert": to_z * per + to_r}, device_id_type=MESH,
                ).start()

            if h == 0 and j == 0:
                pl.when(p != 0)(remote)

                @pl.when(p == 0)
                def _():
                    pltpu.make_async_copy(src, dst, sem).start()

            else:
                remote()

    def pack(i, carry):
        p = at_distance(i)
        to_z = residue(z + n - p, n)
        codes = code_ref[pl.ds(pl.multiple_of(to_z * per, per), per), :]
        slot = iota((per, cap, toks), 1).astype(F32)
        chosen = jnp.where(codes[:, None, :] == slot, 1.0, 0.0).reshape(per * cap, toks)
        block = jnp.dot(chosen.astype(BF16), tok_ref[...], preferred_element_type=F32)
        packed[to_z] = block.astype(BF16).reshape(per, cap, width)
        send_rows(p, 0)
        return carry

    lax.fori_loop(0, n, pack, 0)

    def pack_rest(i, carry):
        send_rows(at_distance(i), 1)
        return carry

    lax.fori_loop(0, n, pack_rest, 0)

    lane = iota((experts, experts * cap), 1)
    spread = jnp.where(lane // cap == iota((experts, experts * cap), 0), 1.0, 0.0).astype(BF16)
    slot_at = jnp.dot(code.T.astype(BF16), spread, preferred_element_type=F32)
    here = slot_at == (iota((toks, experts * cap), 1) % cap).astype(F32)
    weights = picked.T
    high = weights.astype(BF16)
    low = (weights - high.astype(F32)).astype(BF16)
    for k, piece in enumerate((high, low)):
        laid = jnp.dot(piece, spread, preferred_element_type=F32)
        mix_ref[k * toks : (k + 1) * toks, :] = jnp.where(here, laid, 0.0).astype(BF16)

    for load in loads:
        load.wait()

    def await_rows(p, h):
        k = p * 2 + h
        pltpu.make_async_copy(rows.at[k], rows.at[k], pack_recv.at[k]).wait()

    def rows_of(p, h):
        return rows[p * 2 + h].reshape(m_rows, width)

    def reduce_step(h, i, joins):
        k = mid - quotient(i + 1, 2)
        if isinstance(i, int):
            await_rows(residue(y + k, n), h)
            if i:
                await_rows(residue(y + n - k, n), h)
        else:

            @pl.when(residue(i, 2) == 1)
            def _():
                await_rows(residue(y + k, n), h)
                await_rows(residue(y + n - k, n), h)

        for d in (0, 1):
            p = residue(y + (n - k if d else k), n)
            kind = residue(i + d, 2)
            own = rows_of(p, h)
            slot = h * steps + i
            if joins:
                pltpu.make_async_copy(
                    rs_in.at[d, slot - 2], rs_in.at[d, slot - 2], rs_recv.at[d, slot - 2]
                ).wait()
            for f in range(0, ff, tile):
                part = jnp.dot(own, w_buf[kind, :, f : f + tile], preferred_element_type=F32)
                if joins:
                    part = part + rs_in[d, slot - 2, :, f : f + tile].astype(F32)
                rs_out[d, slot, :, f : f + tile] = part.astype(BF16)
            pltpu.make_async_remote_copy(
                src_ref=rs_out.at[d, slot], dst_ref=rs_in.at[d, slot],
                send_sem=rs_send, recv_sem=rs_recv.at[d, slot],
                device_id={"dp": behind if d else ahead}, device_id_type=MESH,
            ).start()

    def reduce_half(h):
        for i in range(2):
            reduce_step(h, i, False)

        def body(i, carry):
            reduce_step(h, i, True)
            return carry

        lax.fori_loop(2, steps, body, 0)

    def finish(h):
        await_rows(y, h)
        last = h * steps + steps - 1
        for d in (0, 1):
            for slot in (last - 1, last):
                pltpu.make_async_copy(
                    rs_in.at[d, slot], rs_in.at[d, slot], rs_recv.at[d, slot]
                ).wait()
        own = rows_of(y, h)
        for f in range(0, ff, tile):
            cut = slice(f, f + tile)
            gate = jnp.dot(own, w_buf[0, :, cut], preferred_element_type=F32)
            gate = gate + rs_in[0, last, :, cut].astype(F32) + rs_in[1, last - 1, :, cut].astype(F32)
            up = jnp.dot(own, w_buf[1, :, cut], preferred_element_type=F32)
            up = up + rs_in[0, last - 1, :, cut].astype(F32) + rs_in[1, last, :, cut].astype(F32)
            hid[h * n + y, :, cut] = (gate / (1.0 + jnp.exp(-gate)) * up).astype(BF16)

    def part_of(h, p, s):
        return hid.at[h * n + p, pl.ds(s * sub_rows, sub_rows)]

    def pass_on(h, s, d, sub):
        part = part_of(h, residue(y + (s if d else n - s), n), sub)
        pltpu.make_async_remote_copy(
            src_ref=part, dst_ref=part, send_sem=ag_send, recv_sem=ag_recv.at[d, h, s, sub],
            device_id={"dp": behind if d else ahead}, device_id_type=MESH,
        ).start()

    def arrived(h, s, d, sub):
        part = part_of(h, residue(y + (s + 1 if d else n - s - 1), n), sub)
        pltpu.make_async_copy(part, part, ag_recv.at[d, h, s, sub]).wait()

    def expert_rows_out(h, p):
        k = h * n + p
        done = jnp.dot(hid[k], d_buf[...], preferred_element_type=F32)
        outs[k] = done.astype(BF16).reshape(half, cap, width)
        to_z = residue(z + p, n)
        for j in range(half):
            dx, dc = divmod(h * half + j, 2)
            to = to_z * per + residue(x + dx, n_x) * 2 + residue(c + dc, 2)
            src, dst = outs.at[k, j], ret.at[me]

            def remote():
                pltpu.make_async_remote_copy(
                    src_ref=src, dst_ref=dst, send_sem=ret_send, recv_sem=ret_recv,
                    device_id={"expert": to}, device_id_type=MESH,
                ).start()

            if h == 0 and j == 0:
                pl.when(p != 0)(remote)

                @pl.when(p == 0)
                def _():
                    pltpu.make_async_copy(src, dst, ret_recv).start()

            else:
                remote()

    def exchange(h, s):
        if s == 0:
            finish(h)
        for sub in (0, 1):
            for d in (0, 1):
                if 0 < s < mid or (s == mid and sub == d):
                    arrived(h, s - 1, d, sub)
                if s < mid - 1 or (s == mid - 1 and sub == d):
                    pass_on(h, s, d, sub)

    def outward(h, s):
        expert_rows_out(h, residue(y + s, n))
        if 0 < s < mid:
            expert_rows_out(h, residue(y + n - s, n))

    reduce_half(0)
    reduce_half(1)
    order = [(0, 0)]
    for s in range(1, mid + 1):
        order += [(0, s), (1, s - 1)]
    order.append((1, mid))
    late = None
    for event in order:
        exchange(*event)
        if late is not None:
            outward(*late)
        late = event
    outward(*late)

    pltpu.make_async_copy(ret, ret, ret_recv).wait()
    back = ret[...].reshape(experts * cap, width)
    mixed = jnp.dot(mix_ref[...], back, preferred_element_type=F32)
    out_ref[...] = (mixed[:toks] + mixed[toks:]).astype(BF16)

    flat = packed.at[0, pl.ds(0, per - 1)]
    pltpu.make_async_copy(flat, flat, pack_send).wait()
    whole = packed.at[pl.ds(0, n - 1)]
    pltpu.make_async_copy(whole, whole, pack_send).wait()
    pltpu.make_async_copy(rs_out, rs_out, rs_send).wait()
    sent = hid.at[pl.ds(0, 2 * n - 2)]
    pltpu.make_async_copy(sent, sent, ag_send).wait()
    back_sent = ret.at[pl.ds(0, experts - 1)]
    pltpu.make_async_copy(back_sent, back_sent, ret_send).wait()


def body(tokens, expert_ids, gate_weights, gate_proj, up_proj, down_proj):
    n, experts = lax.axis_size("dp"), lax.axis_size("expert")
    per = experts // n
    toks, width = tokens.shape
    top = expert_ids.shape[1]
    cap = 2 * toks * top // experts
    ff = gate_proj.shape[2]
    half = per // 2
    m_rows = half * cap
    vmem = pl.BlockSpec(memory_space=pltpu.VMEM)
    hbm = pl.BlockSpec(memory_space=pltpu.HBM)
    flops = 2 * experts * cap * width * ff * 3
    return pl.pallas_call(
        functools.partial(layer, n, per),
        out_shape=jax.ShapeDtypeStruct((toks, width), BF16),
        in_specs=[hbm] * 6,
        out_specs=vmem,
        scratch_shapes=[
            pltpu.VMEM((top, toks), jnp.int32),
            pltpu.VMEM((top, toks), F32),
            pltpu.VMEM((toks, width), BF16),
            pltpu.VMEM((2, width, ff), BF16),
            pltpu.VMEM((ff, width), BF16),
            pltpu.VMEM((experts, toks), F32),
            pltpu.VMEM((2 * toks, experts * cap), BF16),
            pltpu.VMEM((n, per, cap, width), BF16),
            pltpu.VMEM((2 * n, half, cap, width), BF16),
            pltpu.VMEM((2, 2 * (n - 1), m_rows, ff), BF16),
            pltpu.VMEM((2, 2 * (n - 1), m_rows, ff), BF16),
            pltpu.VMEM((2 * n, m_rows, ff), BF16),
            pltpu.VMEM((2 * n, half, cap, width), BF16),
            pltpu.VMEM((experts, cap, width), BF16),
            pltpu.SemaphoreType.DMA((6,)),
            pltpu.SemaphoreType.DMA,
            pltpu.SemaphoreType.DMA((2 * n,)),
            pltpu.SemaphoreType.DMA,
            pltpu.SemaphoreType.DMA((2, 2 * (n - 1))),
            pltpu.SemaphoreType.DMA,
            pltpu.SemaphoreType.DMA((2, 2, n // 2, 2)),
            pltpu.SemaphoreType.DMA,
            pltpu.SemaphoreType.DMA,
        ],
        cost_estimate=pl.CostEstimate(
            flops=flops, bytes_accessed=3 * width * ff * 2, transcendentals=m_rows * 2 * ff
        ),
        compiler_params=pltpu.CompilerParams(
            collective_id=0, has_side_effects=True, vmem_limit_bytes=50 * 2**20
        ),
    )(
        *(
            pltpu.with_memory_space_constraint(a, pltpu.HBM)
            for a in (
                expert_ids.T, gate_weights.T, tokens, gate_proj[0], up_proj[0], down_proj[0]
            )
        )
    )


def solution(mesh):
    placed = (
        P("expert", "dp"),
        P("expert", None),
        P("expert", None),
        P("expert", "dp", None),
        P("expert", "dp", None),
        P("expert", None, "dp"),
    )
    return jax.shard_map(
        body, mesh=mesh, in_specs=placed, out_specs=P("expert", "dp"), check_vma=False
    )
```

```python
import functools

import jax
import jax.numpy as jnp
from jax import lax
from jax.experimental import pallas as pl
from jax.experimental.pallas import tpu as pltpu
from jax.sharding import PartitionSpec as P

MESH = pl.DeviceIdType.MESH
F32 = jnp.float32
BF16 = jnp.bfloat16


def quotient(a, b):
    return a // b if isinstance(a, int) else lax.div(a, jnp.int32(b))


def residue(a, b):
    return a % b if isinstance(a, int) else lax.rem(a, jnp.int32(b))


def z_shifts(n):
    near = sorted(range(n), key=lambda k: -min(k, n - k))
    far = [k for k in near if k != n // 2 and k]
    order = [0, n // 2] + far
    return order[: n // 2], order[n // 2 :]


def iota(shape, dim):
    return lax.broadcasted_iota(jnp.int32, shape, dim)


def layer(
    n, per, ids_hbm, gw_hbm, tok_hbm, gate_hbm, up_hbm, down_hbm, out_ref,
    ids_ref, gw_ref, tok_ref, w_buf, d_buf, code_ref, mix_ref, packed, rows, rs_out, rs_in, hid, outs, ret,
    load_sem, pack_send, pack_recv, rs_send, rs_recv, ag_send, ag_recv, ret_send, ret_recv,
):
    y = lax.axis_index("dp")
    me = lax.axis_index("expert")
    z, r = quotient(me, per), residue(me, per)
    x, c = quotient(r, 2), residue(r, 2)
    n_x, half, mid = per // 2, per // 2, n // 2
    experts = n * per
    top, toks = ids_ref.shape
    width = tok_ref.shape[1]
    cap = packed.shape[2]
    m_rows = half * cap
    ff = w_buf.shape[2]
    tile = min(ff, 512)
    sub_rows = m_rows // 2
    shifts = z_shifts(n)
    ahead, behind = residue(y + 1, n), residue(y + n - 1, n)
    steps = n - 1

    small = [
        pltpu.make_async_copy(ids_hbm, ids_ref, load_sem.at[3]),
        pltpu.make_async_copy(gw_hbm, gw_ref, load_sem.at[4]),
        pltpu.make_async_copy(tok_hbm, tok_ref, load_sem.at[5]),
    ]
    loads = [
        pltpu.make_async_copy(gate_hbm, w_buf.at[0], load_sem.at[0]),
        pltpu.make_async_copy(up_hbm, w_buf.at[1], load_sem.at[1]),
        pltpu.make_async_copy(down_hbm, d_buf, load_sem.at[2]),
    ]
    for load in small:
        load.start()
    barrier = pltpu.get_barrier_semaphore()

    def greet(i, carry):
        pl.semaphore_signal(
            barrier, inc=1, device_id={"expert": residue(me + i, experts)}, device_id_type=MESH
        )
        return carry

    lax.fori_loop(1, experts, greet, 0)
    for to in (ahead, behind):
        pl.semaphore_signal(barrier, inc=1, device_id={"dp": to}, device_id_type=MESH)
    for load in loads:
        load.start()
    for load in small:
        load.wait()

    row = iota((experts, toks), 0)
    expert_of = row % n * per + row // n
    named = jnp.zeros((experts, toks), F32)
    picked = jnp.zeros((experts, toks), F32)
    for k in range(top):
        same = ids_ref[k : k + 1, :] == expert_of
        named = named + jnp.where(same, 1.0, 0.0)
        picked = picked + jnp.where(same, gw_ref[k : k + 1, :], 0.0)
    before = jnp.where(iota((toks, toks), 0) < iota((toks, toks), 1), 1.0, 0.0).astype(BF16)
    earlier = jnp.dot(named.astype(BF16), before, preferred_element_type=F32)
    code = jnp.where(named > 0.0, earlier, -1.0)
    code_ref[...] = code

    pl.semaphore_wait(barrier, experts - 1 + 2)

    def at_distance(i):
        k = mid - quotient(i + 1, 2)
        odd = residue(i, 2)
        return residue(y + odd * k + (1 - odd) * (n - k), n)

    def taker_of(p):
        return residue(x + n_x - quotient(p, 2), n_x) * 2 + residue(c + p, 2)

    def giver_of(p):
        return residue(x + quotient(p, 2), n_x) * 2 + residue(c + p, 2)

    def send_rows(p, h):
        to_r = taker_of(p)
        for j, shift in enumerate(shifts[h]):
            to_z = residue(z + n - shift, n)
            src, dst = packed.at[to_r, to_z], rows.at[p * 2 + h, j]
            sem = pack_recv.at[p * 2 + h]

            def remote():
                pltpu.make_async_remote_copy(
                    src_ref=src, dst_ref=dst, send_sem=pack_send, recv_sem=sem,
                    device_id={"expert": to_z * per + to_r}, device_id_type=MESH,
                ).start()

            if shift == 0:
                pl.when(p != 0)(remote)

                @pl.when(p == 0)
                def _():
                    pltpu.make_async_copy(src, dst, sem).start()

            else:
                remote()

    def pack(i, carry):
        p = at_distance(i)
        to_r = taker_of(p)
        codes = code_ref[pl.ds(pl.multiple_of(to_r * n, n), n), :]
        slot = iota((n, cap, toks), 1).astype(F32)
        chosen = jnp.where(codes[:, None, :] == slot, 1.0, 0.0).reshape(n * cap, toks)
        block = jnp.dot(chosen.astype(BF16), tok_ref[...], preferred_element_type=F32)
        packed[to_r] = block.astype(BF16).reshape(n, cap, width)
        send_rows(p, 0)
        return carry

    lax.fori_loop(0, n, pack, 0)

    for load in loads:
        load.wait()

    def await_rows(p, h):
        k = p * 2 + h
        pltpu.make_async_copy(rows.at[k], rows.at[k], pack_recv.at[k]).wait()

    def rows_of(p, h):
        return rows[p * 2 + h].reshape(m_rows, width)

    def reduce_step(h, i, joins):
        k = mid - quotient(i + 1, 2)
        if isinstance(i, int):
            await_rows(residue(y + k, n), h)
            if i:
                await_rows(residue(y + n - k, n), h)
        else:

            @pl.when(residue(i, 2) == 1)
            def _():
                await_rows(residue(y + k, n), h)
                await_rows(residue(y + n - k, n), h)

        for d in (0, 1):
            p = residue(y + (n - k if d else k), n)
            kind = residue(i + d, 2)
            own = rows_of(p, h)
            slot = h * steps + i
            if joins:
                pltpu.make_async_copy(
                    rs_in.at[d, slot - 2], rs_in.at[d, slot - 2], rs_recv.at[d, slot - 2]
                ).wait()
            for f in range(0, ff, tile):
                part = jnp.dot(own, w_buf[kind, :, f : f + tile], preferred_element_type=F32)
                if joins:
                    part = part + rs_in[d, slot - 2, :, f : f + tile].astype(F32)
                rs_out[d, slot, :, f : f + tile] = part.astype(BF16)
            pltpu.make_async_remote_copy(
                src_ref=rs_out.at[d, slot], dst_ref=rs_in.at[d, slot],
                send_sem=rs_send, recv_sem=rs_recv.at[d, slot],
                device_id={"dp": behind if d else ahead}, device_id_type=MESH,
            ).start()

    def pack_rest(i, carry):
        send_rows(at_distance(i), 1)
        return carry

    def make_mix():
        lane = iota((experts, experts * cap), 1)
        spread = jnp.where(lane // cap == iota((experts, experts * cap), 0), 1.0, 0.0).astype(BF16)
        slot_at = jnp.dot(code_ref[...].T.astype(BF16), spread, preferred_element_type=F32)
        here = slot_at == (iota((toks, experts * cap), 1) % cap).astype(F32)
        weights = picked.T
        high = weights.astype(BF16)
        low = (weights - high.astype(F32)).astype(BF16)
        for k, piece in enumerate((high, low)):
            laid = jnp.dot(piece, spread, preferred_element_type=F32)
            mix_ref[k * toks : (k + 1) * toks, :] = jnp.where(here, laid, 0.0).astype(BF16)

    def reduce_half(h):
        for i in range(2):
            reduce_step(h, i, False)
        if h == 0:
            lax.fori_loop(0, n, pack_rest, 0)

        def body(i, carry):
            reduce_step(h, i, True)
            if h == 1:
                pl.when(i == (steps + 1) // 2)(begin_gather)
            return carry

        lax.fori_loop(2, steps, body, 0)

    def finish(h):
        await_rows(y, h)
        last = h * steps + steps - 1
        for d in (0, 1):
            for slot in (last - 1, last):
                pltpu.make_async_copy(
                    rs_in.at[d, slot], rs_in.at[d, slot], rs_recv.at[d, slot]
                ).wait()
        own = rows_of(y, h)
        for f in range(0, ff, tile):
            cut = slice(f, f + tile)
            gate = jnp.dot(own, w_buf[0, :, cut], preferred_element_type=F32)
            gate = gate + rs_in[0, last, :, cut].astype(F32) + rs_in[1, last - 1, :, cut].astype(F32)
            up = jnp.dot(own, w_buf[1, :, cut], preferred_element_type=F32)
            up = up + rs_in[0, last - 1, :, cut].astype(F32) + rs_in[1, last, :, cut].astype(F32)
            hid[h * n + y, :, cut] = (gate / (1.0 + jnp.exp(-gate)) * up).astype(BF16)

    def part_of(u, p, s, d):
        h, sub = divmod(u, 2)
        if s < mid - 1:
            return hid.at[h * n + p, pl.ds(sub * sub_rows, sub_rows)]
        few = sub_rows // 2
        return hid.at[h * n + p, pl.ds(sub * sub_rows + d * few, few)]

    def pass_on(u, s, d):
        part = part_of(u, residue(y + (s if d else n - s), n), s, d)
        pltpu.make_async_remote_copy(
            src_ref=part, dst_ref=part, send_sem=ag_send, recv_sem=ag_recv.at[d, u, s],
            device_id={"dp": behind if d else ahead}, device_id_type=MESH,
        ).start()

    def arrived(u, s, d):
        part = part_of(u, residue(y + (s + 1 if d else n - s - 1), n), s, d)
        pltpu.make_async_copy(part, part, ag_recv.at[d, u, s]).wait()

    def exchange(u, s):
        for d in (0, 1):
            if s > 0:
                arrived(u, s - 1, d)
            if s < mid:
                pass_on(u, s, d)

    def outward(u, s):
        h, sub = divmod(u, 2)
        pieces = [residue(y + s, n)]
        if 0 < s < mid:
            pieces.append(residue(y + n - s, n))
        keys = [h * n + p for p in pieces]
        cut = slice(sub * sub_rows, (sub + 1) * sub_rows)
        held = jnp.concatenate([hid[k, cut] for k in keys], axis=0)
        done = jnp.dot(held, d_buf[...], preferred_element_type=F32).astype(BF16)
        some = half // 2
        for i, (k, p) in enumerate(zip(keys, pieces)):
            block = done[i * sub_rows : (i + 1) * sub_rows]
            outs[k, sub * some : (sub + 1) * some] = block.reshape(some, cap, width)
            to_r = giver_of(p)
            for j in range(sub * some, (sub + 1) * some):
                shift = shifts[h][j]
                src, dst = outs.at[k, j], ret.at[r * n + z]
                to = residue(z + shift, n) * per + to_r

                def remote():
                    pltpu.make_async_remote_copy(
                        src_ref=src, dst_ref=dst, send_sem=ret_send, recv_sem=ret_recv,
                        device_id={"expert": to}, device_id_type=MESH,
                    ).start()

                if shift == 0:
                    pl.when(p != 0)(remote)

                    @pl.when(p == 0)
                    def _():
                        pltpu.make_async_copy(src, dst, ret_recv).start()

                else:
                    remote()

    def begin_gather():
        finish(0)
        for u in (0, 1):
            exchange(u, 0)
        for u in (0, 1):
            outward(u, 0)

    reduce_half(0)
    make_mix()
    reduce_half(1)
    order = [
        (0, 1), (1, 1), (0, 2), (2, 0), (1, 2), (0, 3), (3, 0), (1, 3), (0, 4), (2, 1),
        (1, 4), (3, 1), (2, 2), (3, 2), (2, 3), (3, 3), (2, 4), (3, 4),
    ]
    late = None
    for u, s in order:
        if s > mid:
            continue
        if s == mid and late:
            outward(*late)
            late = None
        if (u, s) == (2, 0):
            finish(1)
        exchange(u, s)
        if late:
            outward(*late)
        late = (u, s)
    outward(*late)

    pltpu.make_async_copy(ret, ret, ret_recv).wait()
    back = ret[...].reshape(experts * cap, width)
    mixed = jnp.dot(mix_ref[...], back, preferred_element_type=F32)
    out_ref[...] = (mixed[:toks] + mixed[toks:]).astype(BF16)

    flat = packed.at[0, pl.ds(0, per - 1)]
    pltpu.make_async_copy(flat, flat, pack_send).wait()
    whole = packed.at[pl.ds(0, n - 1)]
    pltpu.make_async_copy(whole, whole, pack_send).wait()
    pltpu.make_async_copy(rs_out, rs_out, rs_send).wait()
    sent = hid.at[pl.ds(0, 2 * n - 2)]
    pltpu.make_async_copy(sent, sent, ag_send).wait()
    back_sent = ret.at[pl.ds(0, experts - 1)]
    pltpu.make_async_copy(back_sent, back_sent, ret_send).wait()


def body(tokens, expert_ids, gate_weights, gate_proj, up_proj, down_proj):
    n, experts = lax.axis_size("dp"), lax.axis_size("expert")
    per = experts // n
    assert per == n
    toks, width = tokens.shape
    top = expert_ids.shape[1]
    cap = 2 * toks * top // experts
    ff = gate_proj.shape[2]
    half = per // 2
    m_rows = half * cap
    vmem = pl.BlockSpec(memory_space=pltpu.VMEM)
    hbm = pl.BlockSpec(memory_space=pltpu.HBM)
    flops = 2 * experts * cap * width * ff * 3
    return pl.pallas_call(
        functools.partial(layer, n, per),
        out_shape=jax.ShapeDtypeStruct((toks, width), BF16),
        in_specs=[hbm] * 6,
        out_specs=vmem,
        scratch_shapes=[
            pltpu.VMEM((top, toks), jnp.int32),
            pltpu.VMEM((top, toks), F32),
            pltpu.VMEM((toks, width), BF16),
            pltpu.VMEM((2, width, ff), BF16),
            pltpu.VMEM((ff, width), BF16),
            pltpu.VMEM((experts, toks), F32),
            pltpu.VMEM((2 * toks, experts * cap), BF16),
            pltpu.VMEM((n, per, cap, width), BF16),
            pltpu.VMEM((2 * n, half, cap, width), BF16),
            pltpu.VMEM((2, 2 * (n - 1), m_rows, ff), BF16),
            pltpu.VMEM((2, 2 * (n - 1), m_rows, ff), BF16),
            pltpu.VMEM((2 * n, m_rows, ff), BF16),
            pltpu.VMEM((2 * n, half, cap, width), BF16),
            pltpu.VMEM((experts, cap, width), BF16),
            pltpu.SemaphoreType.DMA((6,)),
            pltpu.SemaphoreType.DMA,
            pltpu.SemaphoreType.DMA((2 * n,)),
            pltpu.SemaphoreType.DMA,
            pltpu.SemaphoreType.DMA((2, 2 * (n - 1))),
            pltpu.SemaphoreType.DMA,
            pltpu.SemaphoreType.DMA((2, 4, n // 2)),
            pltpu.SemaphoreType.DMA,
            pltpu.SemaphoreType.DMA,
        ],
        cost_estimate=pl.CostEstimate(
            flops=flops, bytes_accessed=3 * width * ff * 2, transcendentals=m_rows * 2 * ff
        ),
        compiler_params=pltpu.CompilerParams(
            collective_id=0, has_side_effects=True, vmem_limit_bytes=50 * 2**20
        ),
    )(
        *(
            pltpu.with_memory_space_constraint(a, pltpu.HBM)
            for a in (
                expert_ids.T, gate_weights.T, tokens, gate_proj[0], up_proj[0], down_proj[0]
            )
        )
    )


def solution(mesh):
    placed = (
        P("expert", "dp"),
        P("expert", None),
        P("expert", None),
        P("expert", "dp", None),
        P("expert", "dp", None),
        P("expert", None, "dp"),
    )
    return jax.shard_map(
        body, mesh=mesh, in_specs=placed, out_specs=P("expert", "dp"), check_vma=False
    )
```

```python
import functools

import jax
import jax.numpy as jnp
from jax import lax
from jax.experimental import pallas as pl
from jax.experimental.pallas import tpu as pltpu
from jax.sharding import PartitionSpec as P

MESH = pl.DeviceIdType.MESH
F32 = jnp.float32
BF16 = jnp.bfloat16


def quotient(a, b):
    return a // b if isinstance(a, int) else lax.div(a, jnp.int32(b))


def residue(a, b):
    return a % b if isinstance(a, int) else lax.rem(a, jnp.int32(b))


def z_shifts(n):
    order = sorted(range(n), key=lambda k: min(k, n - k))
    near, far = order[: n // 2], order[n // 2 :]
    return near[:1] + near[-1:] + near[1:-1], far[-1:] + far[:-1]


def iota(shape, dim):
    return lax.broadcasted_iota(jnp.int32, shape, dim)


def layer(
    n, per, ids_hbm, gw_hbm, tok_hbm, gate_hbm, up_hbm, down_hbm, out_ref,
    ids_ref, gw_ref, tok_ref, w_buf, d_buf, code_ref, mix_ref, packed, rows, rs_out, rs_in, hid, outs, ret,
    load_sem, pack_send, pack_recv, rs_send, rs_recv, ag_send, ag_recv, ret_send, ret_recv,
):
    y = lax.axis_index("dp")
    me = lax.axis_index("expert")
    z, r = quotient(me, per), residue(me, per)
    x, c = quotient(r, 2), residue(r, 2)
    n_x, half, mid = per // 2, per // 2, n // 2
    experts = n * per
    top, toks = ids_ref.shape
    width = tok_ref.shape[1]
    cap = packed.shape[2]
    m_rows = half * cap
    ff = w_buf.shape[2]
    tile = min(ff, 512)
    sub_rows = m_rows // 2
    shifts = z_shifts(n)
    ahead, behind = residue(y + 1, n), residue(y + n - 1, n)
    steps = n - 1

    small = [
        pltpu.make_async_copy(ids_hbm, ids_ref, load_sem.at[3]),
        pltpu.make_async_copy(gw_hbm, gw_ref, load_sem.at[4]),
        pltpu.make_async_copy(tok_hbm, tok_ref, load_sem.at[5]),
    ]
    loads = [
        pltpu.make_async_copy(gate_hbm, w_buf.at[0], load_sem.at[0]),
        pltpu.make_async_copy(up_hbm, w_buf.at[1], load_sem.at[1]),
        pltpu.make_async_copy(down_hbm, d_buf, load_sem.at[2]),
    ]
    for load in small + loads:
        load.start()
    barrier = pltpu.get_barrier_semaphore()

    def greet(i, carry):
        pl.semaphore_signal(
            barrier, inc=1, device_id={"expert": residue(me + i, experts)}, device_id_type=MESH
        )
        return carry

    lax.fori_loop(1, experts, greet, 0)
    for to in (ahead, behind):
        pl.semaphore_signal(barrier, inc=1, device_id={"dp": to}, device_id_type=MESH)
    for load in small:
        load.wait()

    row = iota((experts, toks), 0)
    expert_of = row % n * per + row // n
    named = jnp.zeros((experts, toks), F32)
    picked = jnp.zeros((experts, toks), F32)
    for k in range(top):
        same = ids_ref[k : k + 1, :] == expert_of
        named = named + jnp.where(same, 1.0, 0.0)
        picked = picked + jnp.where(same, gw_ref[k : k + 1, :], 0.0)
    before = jnp.where(iota((toks, toks), 0) < iota((toks, toks), 1), 1.0, 0.0).astype(BF16)
    earlier = jnp.dot(named.astype(BF16), before, preferred_element_type=F32)
    code = jnp.where(named > 0.0, earlier, -1.0)
    code_ref[...] = code

    pl.semaphore_wait(barrier, experts - 1 + 2)

    def at_distance(i):
        k = mid - quotient(i + 1, 2)
        odd = residue(i, 2)
        return residue(y + odd * k + (1 - odd) * (n - k), n)

    def taker_of(p):
        return residue(x + n_x - quotient(p, 2), n_x) * 2 + residue(c + p, 2)

    def giver_of(p):
        return residue(x + quotient(p, 2), n_x) * 2 + residue(c + p, 2)

    def send_rows(p, h):
        to_r = taker_of(p)
        for j, shift in enumerate(shifts[h]):
            to_z = residue(z + n - shift, n)
            src, dst = packed.at[to_r, to_z], rows.at[p * 2 + h, j]
            sem = pack_recv.at[p * 2 + h]

            def remote():
                pltpu.make_async_remote_copy(
                    src_ref=src, dst_ref=dst, send_sem=pack_send, recv_sem=sem,
                    device_id={"expert": to_z * per + to_r}, device_id_type=MESH,
                ).start()

            if shift == 0:
                pl.when(p != 0)(remote)

                @pl.when(p == 0)
                def _():
                    pltpu.make_async_copy(src, dst, sem).start()

            else:
                remote()

    def pack(i, carry):
        p = at_distance(i)
        to_r = taker_of(p)
        codes = code_ref[pl.ds(pl.multiple_of(to_r * n, n), n), :]
        slot = iota((n, cap, toks), 1).astype(F32)
        chosen = jnp.where(codes[:, None, :] == slot, 1.0, 0.0).reshape(n * cap, toks)
        block = jnp.dot(chosen.astype(BF16), tok_ref[...], preferred_element_type=F32)
        packed[to_r] = block.astype(BF16).reshape(n, cap, width)
        send_rows(p, 0)
        return carry

    lax.fori_loop(0, n // 2, pack, 0)
    for load in loads[:2]:
        load.wait()

    def await_rows(p, h):
        k = p * 2 + h
        pltpu.make_async_copy(rows.at[k], rows.at[k], pack_recv.at[k]).wait()

    def rows_of(p, h):
        return rows[p * 2 + h].reshape(m_rows, width)

    def reduce_step(h, i, joins):
        k = mid - quotient(i + 1, 2)
        if isinstance(i, int):
            await_rows(residue(y + k, n), h)
            if i:
                await_rows(residue(y + n - k, n), h)
        else:

            @pl.when(residue(i, 2) == 1)
            def _():
                await_rows(residue(y + k, n), h)
                await_rows(residue(y + n - k, n), h)

        for d in (0, 1):
            p = residue(y + (n - k if d else k), n)
            kind = residue(i + d, 2)
            own = rows_of(p, h)
            slot = h * steps + i
            if joins:
                pltpu.make_async_copy(
                    rs_in.at[d, slot - 2], rs_in.at[d, slot - 2], rs_recv.at[d, slot - 2]
                ).wait()
            for f in range(0, ff, tile):
                part = jnp.dot(own, w_buf[kind, :, f : f + tile], preferred_element_type=F32)
                if joins:
                    part = part + rs_in[d, slot - 2, :, f : f + tile].astype(F32)
                rs_out[d, slot, :, f : f + tile] = part.astype(BF16)
            pltpu.make_async_remote_copy(
                src_ref=rs_out.at[d, slot], dst_ref=rs_in.at[d, slot],
                send_sem=rs_send, recv_sem=rs_recv.at[d, slot],
                device_id={"dp": behind if d else ahead}, device_id_type=MESH,
            ).start()

    def pack_rest(i, carry):
        send_rows(at_distance(i), 1)
        return carry

    def make_mix():
        lane = iota((experts, experts * cap), 1)
        spread = jnp.where(lane // cap == iota((experts, experts * cap), 0), 1.0, 0.0).astype(BF16)
        slot_at = jnp.dot(code_ref[...].T.astype(BF16), spread, preferred_element_type=F32)
        here = slot_at == (iota((toks, experts * cap), 1) % cap).astype(F32)
        weights = picked.T
        high = weights.astype(BF16)
        low = (weights - high.astype(F32)).astype(BF16)
        for k, piece in enumerate((high, low)):
            laid = jnp.dot(piece, spread, preferred_element_type=F32)
            mix_ref[k * toks : (k + 1) * toks, :] = jnp.where(here, laid, 0.0).astype(BF16)

    def reduce_half(h):
        for i in range(2):
            reduce_step(h, i, False)
            if (h, i) == (0, 0):
                lax.fori_loop(n // 2, n, pack, 0)
        if h == 0:
            lax.fori_loop(0, n, pack_rest, 0)
            loads[2].wait()

        def body(i, carry):
            reduce_step(h, i, True)
            if h == 1:
                pl.when(i == (steps + 1) // 2)(begin_gather)
            return carry

        lax.fori_loop(2, steps, body, 0)

    def finish(h):
        await_rows(y, h)
        last = h * steps + steps - 1
        for d in (0, 1):
            for slot in (last - 1, last):
                pltpu.make_async_copy(
                    rs_in.at[d, slot], rs_in.at[d, slot], rs_recv.at[d, slot]
                ).wait()
        own = rows_of(y, h)
        for f in range(0, ff, tile):
            cut = slice(f, f + tile)
            gate = jnp.dot(own, w_buf[0, :, cut], preferred_element_type=F32)
            gate = gate + rs_in[0, last, :, cut].astype(F32) + rs_in[1, last - 1, :, cut].astype(F32)
            up = jnp.dot(own, w_buf[1, :, cut], preferred_element_type=F32)
            up = up + rs_in[0, last - 1, :, cut].astype(F32) + rs_in[1, last, :, cut].astype(F32)
            hid[h * n + y, :, cut] = (gate / (1.0 + jnp.exp(-gate)) * up).astype(BF16)

    def part_of(u, p, s, d):
        h, sub = divmod(u, 2)
        if s < mid - 1:
            return hid.at[h * n + p, pl.ds(sub * sub_rows, sub_rows)]
        few = sub_rows // 2
        return hid.at[h * n + p, pl.ds(sub * sub_rows + d * few, few)]

    def pass_on(u, s, d):
        part = part_of(u, residue(y + (s if d else n - s), n), s, d)
        pltpu.make_async_remote_copy(
            src_ref=part, dst_ref=part, send_sem=ag_send, recv_sem=ag_recv.at[d, u, s],
            device_id={"dp": behind if d else ahead}, device_id_type=MESH,
        ).start()

    def arrived(u, s, d):
        part = part_of(u, residue(y + (s + 1 if d else n - s - 1), n), s, d)
        pltpu.make_async_copy(part, part, ag_recv.at[d, u, s]).wait()

    def exchange(u, s):
        for d in (0, 1):
            if s > 0:
                arrived(u, s - 1, d)
            if s < mid:
                pass_on(u, s, d)

    def outward(u, s):
        h, sub = divmod(u, 2)
        pieces = [residue(y + s, n)]
        if 0 < s < mid:
            pieces.append(residue(y + n - s, n))
        keys = [h * n + p for p in pieces]
        cut = slice(sub * sub_rows, (sub + 1) * sub_rows)
        held = jnp.concatenate([hid[k, cut] for k in keys], axis=0)
        done = jnp.dot(held, d_buf[...], preferred_element_type=F32).astype(BF16)
        some = half // 2
        for i, (k, p) in enumerate(zip(keys, pieces)):
            block = done[i * sub_rows : (i + 1) * sub_rows]
            outs[k, sub * some : (sub + 1) * some] = block.reshape(some, cap, width)
            to_r = giver_of(p)
            for j in range(sub * some, (sub + 1) * some):
                shift = shifts[h][j]
                src, dst = outs.at[k, j], ret.at[r * n + z]
                to = residue(z + shift, n) * per + to_r

                def remote():
                    pltpu.make_async_remote_copy(
                        src_ref=src, dst_ref=dst, send_sem=ret_send, recv_sem=ret_recv,
                        device_id={"expert": to}, device_id_type=MESH,
                    ).start()

                if shift == 0:
                    pl.when(p != 0)(remote)

                    @pl.when(p == 0)
                    def _():
                        pltpu.make_async_copy(src, dst, ret_recv).start()

                else:
                    remote()

    def begin_gather():
        finish(0)
        exchange(0, 0)
        outward(0, 0)

    reduce_half(0)
    make_mix()
    reduce_half(1)
    order = [
        (0, 1), (1, 0), (2, 0), (0, 2), (3, 0), (2, 1), (0, 3), (3, 1), (2, 2), (0, 4),
        (1, 1), (3, 2), (2, 3), (1, 2), (3, 3), (2, 4), (1, 3), (3, 4), (1, 4),
    ]
    late = None
    for u, s in order:
        if s > mid:
            continue
        if s == mid and late:
            outward(*late)
            late = None
        if (u, s) == (2, 0):
            finish(1)
        exchange(u, s)
        if late:
            outward(*late)
        late = (u, s)
    outward(*late)

    pltpu.make_async_copy(ret, ret, ret_recv).wait()
    back = ret[...].reshape(experts * cap, width)
    mixed = jnp.dot(mix_ref[...], back, preferred_element_type=F32)
    out_ref[...] = (mixed[:toks] + mixed[toks:]).astype(BF16)

    flat = packed.at[0, pl.ds(0, per - 1)]
    pltpu.make_async_copy(flat, flat, pack_send).wait()
    whole = packed.at[pl.ds(0, n - 1)]
    pltpu.make_async_copy(whole, whole, pack_send).wait()
    pltpu.make_async_copy(rs_out, rs_out, rs_send).wait()
    sent = hid.at[pl.ds(0, 2 * n - 2)]
    pltpu.make_async_copy(sent, sent, ag_send).wait()
    back_sent = ret.at[pl.ds(0, experts - 1)]
    pltpu.make_async_copy(back_sent, back_sent, ret_send).wait()


def body(tokens, expert_ids, gate_weights, gate_proj, up_proj, down_proj):
    n, experts = lax.axis_size("dp"), lax.axis_size("expert")
    per = experts // n
    assert per == n
    toks, width = tokens.shape
    top = expert_ids.shape[1]
    cap = 2 * toks * top // experts
    ff = gate_proj.shape[2]
    half = per // 2
    m_rows = half * cap
    vmem = pl.BlockSpec(memory_space=pltpu.VMEM)
    hbm = pl.BlockSpec(memory_space=pltpu.HBM)
    flops = 2 * experts * cap * width * ff * 3
    return pl.pallas_call(
        functools.partial(layer, n, per),
        out_shape=jax.ShapeDtypeStruct((toks, width), BF16),
        in_specs=[hbm] * 6,
        out_specs=vmem,
        scratch_shapes=[
            pltpu.VMEM((top, toks), jnp.int32),
            pltpu.VMEM((top, toks), F32),
            pltpu.VMEM((toks, width), BF16),
            pltpu.VMEM((2, width, ff), BF16),
            pltpu.VMEM((ff, width), BF16),
            pltpu.VMEM((experts, toks), F32),
            pltpu.VMEM((2 * toks, experts * cap), BF16),
            pltpu.VMEM((n, per, cap, width), BF16),
            pltpu.VMEM((2 * n, half, cap, width), BF16),
            pltpu.VMEM((2, 2 * (n - 1), m_rows, ff), BF16),
            pltpu.VMEM((2, 2 * (n - 1), m_rows, ff), BF16),
            pltpu.VMEM((2 * n, m_rows, ff), BF16),
            pltpu.VMEM((2 * n, half, cap, width), BF16),
            pltpu.VMEM((experts, cap, width), BF16),
            pltpu.SemaphoreType.DMA((6,)),
            pltpu.SemaphoreType.DMA,
            pltpu.SemaphoreType.DMA((2 * n,)),
            pltpu.SemaphoreType.DMA,
            pltpu.SemaphoreType.DMA((2, 2 * (n - 1))),
            pltpu.SemaphoreType.DMA,
            pltpu.SemaphoreType.DMA((2, 4, n // 2)),
            pltpu.SemaphoreType.DMA,
            pltpu.SemaphoreType.DMA,
        ],
        cost_estimate=pl.CostEstimate(
            flops=flops, bytes_accessed=3 * width * ff * 2, transcendentals=m_rows * 2 * ff
        ),
        compiler_params=pltpu.CompilerParams(
            collective_id=0, has_side_effects=True, vmem_limit_bytes=50 * 2**20
        ),
    )(
        *(
            pltpu.with_memory_space_constraint(a, pltpu.HBM)
            for a in (
                expert_ids.T, gate_weights.T, tokens, gate_proj[0], up_proj[0], down_proj[0]
            )
        )
    )


def solution(mesh):
    placed = (
        P("expert", "dp"),
        P("expert", None),
        P("expert", None),
        P("expert", "dp", None),
        P("expert", "dp", None),
        P("expert", None, "dp"),
    )
    return jax.shard_map(
        body, mesh=mesh, in_specs=placed, out_specs=P("expert", "dp"), check_vma=False
    )
```

```python
import functools

import jax
import jax.numpy as jnp
from jax import lax
from jax.experimental import pallas as pl
from jax.experimental.pallas import tpu as pltpu
from jax.sharding import PartitionSpec as P

MESH = pl.DeviceIdType.MESH
F32 = jnp.float32
BF16 = jnp.bfloat16


def quotient(a, b):
    return a // b if isinstance(a, int) else lax.div(a, jnp.int32(b))


def residue(a, b):
    return a % b if isinstance(a, int) else lax.rem(a, jnp.int32(b))


def z_shifts(n):
    order = sorted(range(n), key=lambda k: min(k, n - k))
    near, far = order[: n // 2], order[n // 2 :]
    return near[:1] + near[-1:] + near[1:-1], far[-1:] + far[:-1]


def iota(shape, dim):
    return lax.broadcasted_iota(jnp.int32, shape, dim)


def layer(
    n, per, ids_hbm, gw_hbm, tok_hbm, gate_hbm, up_hbm, down_hbm, out_ref,
    ids_ref, gw_ref, tok_ref, w_buf, d_buf, code_ref, mix_ref, packed, rows, parts, rs_out, rs_in, hid, outs, ret,
    load_sem, pack_send, pack_recv, rs_send, rs_recv, ag_send, ag_recv, ret_send, ret_recv,
):
    y = lax.axis_index("dp")
    me = lax.axis_index("expert")
    z, r = quotient(me, per), residue(me, per)
    x, c = quotient(r, 2), residue(r, 2)
    n_x, half, mid = per // 2, per // 2, n // 2
    experts = n * per
    top, toks = ids_ref.shape
    width = tok_ref.shape[1]
    cap = packed.shape[2]
    m_rows = half * cap
    ff = w_buf.shape[2]
    tile = min(ff, 512)
    sub_rows = m_rows // 2
    shifts = z_shifts(n)
    ahead, behind = residue(y + 1, n), residue(y + n - 1, n)
    steps = n - 1

    small = [
        pltpu.make_async_copy(ids_hbm, ids_ref, load_sem.at[3]),
        pltpu.make_async_copy(gw_hbm, gw_ref, load_sem.at[4]),
        pltpu.make_async_copy(tok_hbm, tok_ref, load_sem.at[5]),
    ]
    loads = [
        pltpu.make_async_copy(gate_hbm, w_buf.at[0], load_sem.at[0]),
        pltpu.make_async_copy(up_hbm, w_buf.at[1], load_sem.at[1]),
        pltpu.make_async_copy(down_hbm, d_buf, load_sem.at[2]),
    ]
    for load in small + loads:
        load.start()
    barrier = pltpu.get_barrier_semaphore()

    def greet(i, carry):
        pl.semaphore_signal(
            barrier, inc=1, device_id={"expert": residue(me + i, experts)}, device_id_type=MESH
        )
        return carry

    lax.fori_loop(1, experts, greet, 0)
    for to in (ahead, behind):
        pl.semaphore_signal(barrier, inc=1, device_id={"dp": to}, device_id_type=MESH)
    for load in small:
        load.wait()

    row = iota((experts, toks), 0)
    expert_of = row % n * per + row // n
    named = jnp.zeros((experts, toks), F32)
    picked = jnp.zeros((experts, toks), F32)
    for k in range(top):
        same = ids_ref[k : k + 1, :] == expert_of
        named = named + jnp.where(same, 1.0, 0.0)
        picked = picked + jnp.where(same, gw_ref[k : k + 1, :], 0.0)
    before = jnp.where(iota((toks, toks), 0) < iota((toks, toks), 1), 1.0, 0.0).astype(BF16)
    earlier = jnp.dot(named.astype(BF16), before, preferred_element_type=F32)
    code = jnp.where(named > 0.0, earlier, -1.0)
    code_ref[...] = code

    pl.semaphore_wait(barrier, experts - 1 + 2)

    def at_distance(i):
        k = mid - quotient(i + 1, 2)
        odd = residue(i, 2)
        return residue(y + odd * k + (1 - odd) * (n - k), n)

    def taker_of(p):
        return residue(x + n_x - quotient(p, 2), n_x) * 2 + residue(c + p, 2)

    def giver_of(p):
        return residue(x + quotient(p, 2), n_x) * 2 + residue(c + p, 2)

    def send_rows(p, h):
        to_r = taker_of(p)
        for j, shift in enumerate(shifts[h]):
            to_z = residue(z + n - shift, n)
            src, dst = packed.at[to_r, to_z], rows.at[p * 2 + h, j]
            sem = pack_recv.at[p * 2 + h]

            def remote():
                pltpu.make_async_remote_copy(
                    src_ref=src, dst_ref=dst, send_sem=pack_send, recv_sem=sem,
                    device_id={"expert": to_z * per + to_r}, device_id_type=MESH,
                ).start()

            if shift == 0:
                pl.when(p != 0)(remote)

                @pl.when(p == 0)
                def _():
                    pltpu.make_async_copy(src, dst, sem).start()

            else:
                remote()

    def pack(i, carry):
        p = at_distance(i)
        to_r = taker_of(p)
        codes = code_ref[pl.ds(pl.multiple_of(to_r * n, n), n), :]
        slot = iota((n, cap, toks), 1).astype(F32)
        chosen = jnp.where(codes[:, None, :] == slot, 1.0, 0.0).reshape(n * cap, toks)
        block = jnp.dot(chosen.astype(BF16), tok_ref[...], preferred_element_type=F32)
        packed[to_r] = block.astype(BF16).reshape(n, cap, width)
        send_rows(p, 0)
        return carry

    lax.fori_loop(0, n // 2, pack, 0)
    for load in loads[:2]:
        load.wait()

    def await_rows(p, h):
        k = p * 2 + h
        pltpu.make_async_copy(rows.at[k], rows.at[k], pack_recv.at[k]).wait()

    def rows_of(p, h):
        return rows[p * 2 + h].reshape(m_rows, width)

    def send_sums(d, slot):
        pltpu.make_async_remote_copy(
            src_ref=rs_out.at[d, slot], dst_ref=rs_in.at[d, slot],
            send_sem=rs_send, recv_sem=rs_recv.at[d, slot],
            device_id={"dp": behind if d else ahead}, device_id_type=MESH,
        ).start()

    def reduce_step(h, i, joins):
        k = mid - quotient(i + 1, 2)
        if isinstance(i, int):
            await_rows(residue(y + k, n), h)
            if i:
                await_rows(residue(y + n - k, n), h)
        else:

            @pl.when(residue(i, 2) == 1)
            def _():
                await_rows(residue(y + k, n), h)
                await_rows(residue(y + n - k, n), h)

        slot = h * steps + i
        for d in (0, 1):
            own = rows_of(residue(y + (n - k if d else k), n), h)
            kind = residue(i + d, 2)
            for f in range(0, ff, tile):
                cut = slice(f, f + tile)
                part = jnp.dot(own, w_buf[kind, :, cut], preferred_element_type=F32)
                if joins:
                    parts[d, :, cut] = part
                else:
                    rs_out[d, slot, :, cut] = part.astype(BF16)
            if not joins:
                send_sums(d, slot)
        if joins:
            for d in (0, 1):
                came = rs_in.at[d, slot - 2]
                pltpu.make_async_copy(came, came, rs_recv.at[d, slot - 2]).wait()
                rs_out[d, slot] = (parts[d] + came[...].astype(F32)).astype(BF16)
                send_sums(d, slot)

    def pack_rest(i, carry):
        send_rows(at_distance(i), 1)
        return carry

    def make_mix():
        lane = iota((experts, experts * cap), 1)
        spread = jnp.where(lane // cap == iota((experts, experts * cap), 0), 1.0, 0.0).astype(BF16)
        slot_at = jnp.dot(code_ref[...].T.astype(BF16), spread, preferred_element_type=F32)
        here = slot_at == (iota((toks, experts * cap), 1) % cap).astype(F32)
        weights = picked.T
        high = weights.astype(BF16)
        low = (weights - high.astype(F32)).astype(BF16)
        for k, piece in enumerate((high, low)):
            laid = jnp.dot(piece, spread, preferred_element_type=F32)
            mix_ref[k * toks : (k + 1) * toks, :] = jnp.where(here, laid, 0.0).astype(BF16)

    def reduce_half(h):
        for i in range(2):
            reduce_step(h, i, False)
            if (h, i) == (0, 0):
                lax.fori_loop(n // 2, n, pack, 0)
        if h == 0:
            lax.fori_loop(0, n // 2, pack_rest, 0)
            loads[2].wait()

        def body(i, carry):
            reduce_step(h, i, True)
            if h == 0:

                @pl.when(i == 2)
                def _():
                    lax.fori_loop(n // 2, n, pack_rest, 0)

            else:
                pl.when(i == (steps + 1) // 2)(begin_gather)
            return carry

        lax.fori_loop(2, steps, body, 0)

    def finish(h):
        await_rows(y, h)
        own = rows_of(y, h)
        for kind in (0, 1):
            for f in range(0, ff, tile):
                cut = slice(f, f + tile)
                parts[kind, :, cut] = jnp.dot(
                    own, w_buf[kind, :, cut], preferred_element_type=F32
                )
        last = h * steps + steps - 1
        for d in (0, 1):
            for slot in (last - 1, last):
                pltpu.make_async_copy(
                    rs_in.at[d, slot], rs_in.at[d, slot], rs_recv.at[d, slot]
                ).wait()
        for f in range(0, ff, tile):
            cut = slice(f, f + tile)
            gate = parts[0, :, cut] + rs_in[0, last, :, cut].astype(F32)
            gate = gate + rs_in[1, last - 1, :, cut].astype(F32)
            up = parts[1, :, cut] + rs_in[0, last - 1, :, cut].astype(F32)
            up = up + rs_in[1, last, :, cut].astype(F32)
            hid[h * n + y, :, cut] = (gate / (1.0 + jnp.exp(-gate)) * up).astype(BF16)

    def part_of(u, p, s, d):
        h, sub = divmod(u, 2)
        if s < mid - 1:
            return hid.at[h * n + p, pl.ds(sub * sub_rows, sub_rows)]
        few = sub_rows // 2
        return hid.at[h * n + p, pl.ds(sub * sub_rows + d * few, few)]

    def pass_on(u, s, d):
        part = part_of(u, residue(y + (s if d else n - s), n), s, d)
        pltpu.make_async_remote_copy(
            src_ref=part, dst_ref=part, send_sem=ag_send, recv_sem=ag_recv.at[d, u, s],
            device_id={"dp": behind if d else ahead}, device_id_type=MESH,
        ).start()

    def arrived(u, s, d):
        part = part_of(u, residue(y + (s + 1 if d else n - s - 1), n), s, d)
        pltpu.make_async_copy(part, part, ag_recv.at[d, u, s]).wait()

    def exchange(u, s):
        for d in (0, 1):
            if s > 0:
                arrived(u, s - 1, d)
            if s < mid:
                pass_on(u, s, d)

    def outward(u, s):
        h, sub = divmod(u, 2)
        pieces = [residue(y + s, n)]
        if 0 < s < mid:
            pieces.append(residue(y + n - s, n))
        keys = [h * n + p for p in pieces]
        cut = slice(sub * sub_rows, (sub + 1) * sub_rows)
        held = jnp.concatenate([hid[k, cut] for k in keys], axis=0)
        done = jnp.dot(held, d_buf[...], preferred_element_type=F32).astype(BF16)
        some = half // 2
        for i, (k, p) in enumerate(zip(keys, pieces)):
            block = done[i * sub_rows : (i + 1) * sub_rows]
            outs[k, sub * some : (sub + 1) * some] = block.reshape(some, cap, width)
            to_r = giver_of(p)
            for j in range(sub * some, (sub + 1) * some):
                shift = shifts[h][j]
                src, dst = outs.at[k, j], ret.at[r * n + z]
                to = residue(z + shift, n) * per + to_r

                def remote():
                    pltpu.make_async_remote_copy(
                        src_ref=src, dst_ref=dst, send_sem=ret_send, recv_sem=ret_recv,
                        device_id={"expert": to}, device_id_type=MESH,
                    ).start()

                if shift == 0:
                    pl.when(p != 0)(remote)

                    @pl.when(p == 0)
                    def _():
                        pltpu.make_async_copy(src, dst, ret_recv).start()

                else:
                    remote()

    def begin_gather():
        finish(0)
        exchange(0, 0)
        outward(0, 0)

    reduce_half(0)
    make_mix()
    reduce_half(1)
    order = [
        (0, 1), (1, 0), (2, 0), (0, 2), (3, 0), (2, 1), (0, 3), (3, 1), (2, 2), (0, 4),
        (1, 1), (3, 2), (2, 3), (1, 2), (3, 3), (2, 4), (1, 3), (3, 4), (1, 4),
    ]
    late = None
    for u, s in order:
        if s > mid:
            continue
        if s == mid and late:
            outward(*late)
            late = None
        if (u, s) == (2, 0):
            finish(1)
        exchange(u, s)
        if late:
            outward(*late)
        late = (u, s)
    outward(*late)

    pltpu.make_async_copy(ret, ret, ret_recv).wait()
    back = ret[...].reshape(experts * cap, width)
    mixed = jnp.dot(mix_ref[...], back, preferred_element_type=F32)
    out_ref[...] = (mixed[:toks] + mixed[toks:]).astype(BF16)

    flat = packed.at[0, pl.ds(0, per - 1)]
    pltpu.make_async_copy(flat, flat, pack_send).wait()
    whole = packed.at[pl.ds(0, n - 1)]
    pltpu.make_async_copy(whole, whole, pack_send).wait()
    pltpu.make_async_copy(rs_out, rs_out, rs_send).wait()
    sent = hid.at[pl.ds(0, 2 * n - 2)]
    pltpu.make_async_copy(sent, sent, ag_send).wait()
    back_sent = ret.at[pl.ds(0, experts - 1)]
    pltpu.make_async_copy(back_sent, back_sent, ret_send).wait()


def body(tokens, expert_ids, gate_weights, gate_proj, up_proj, down_proj):
    n, experts = lax.axis_size("dp"), lax.axis_size("expert")
    per = experts // n
    assert per == n
    toks, width = tokens.shape
    top = expert_ids.shape[1]
    cap = 2 * toks * top // experts
    ff = gate_proj.shape[2]
    half = per // 2
    m_rows = half * cap
    vmem = pl.BlockSpec(memory_space=pltpu.VMEM)
    hbm = pl.BlockSpec(memory_space=pltpu.HBM)
    flops = 2 * experts * cap * width * ff * 3
    return pl.pallas_call(
        functools.partial(layer, n, per),
        out_shape=jax.ShapeDtypeStruct((toks, width), BF16),
        in_specs=[hbm] * 6,
        out_specs=vmem,
        scratch_shapes=[
            pltpu.VMEM((top, toks), jnp.int32),
            pltpu.VMEM((top, toks), F32),
            pltpu.VMEM((toks, width), BF16),
            pltpu.VMEM((2, width, ff), BF16),
            pltpu.VMEM((ff, width), BF16),
            pltpu.VMEM((experts, toks), F32),
            pltpu.VMEM((2 * toks, experts * cap), BF16),
            pltpu.VMEM((n, per, cap, width), BF16),
            pltpu.VMEM((2 * n, half, cap, width), BF16),
            pltpu.VMEM((2, m_rows, ff), F32),
            pltpu.VMEM((2, 2 * (n - 1), m_rows, ff), BF16),
            pltpu.VMEM((2, 2 * (n - 1), m_rows, ff), BF16),
            pltpu.VMEM((2 * n, m_rows, ff), BF16),
            pltpu.VMEM((2 * n, half, cap, width), BF16),
            pltpu.VMEM((experts, cap, width), BF16),
            pltpu.SemaphoreType.DMA((6,)),
            pltpu.SemaphoreType.DMA,
            pltpu.SemaphoreType.DMA((2 * n,)),
            pltpu.SemaphoreType.DMA,
            pltpu.SemaphoreType.DMA((2, 2 * (n - 1))),
            pltpu.SemaphoreType.DMA,
            pltpu.SemaphoreType.DMA((2, 4, n // 2)),
            pltpu.SemaphoreType.DMA,
            pltpu.SemaphoreType.DMA,
        ],
        cost_estimate=pl.CostEstimate(
            flops=flops, bytes_accessed=3 * width * ff * 2, transcendentals=m_rows * 2 * ff
        ),
        compiler_params=pltpu.CompilerParams(
            collective_id=0, has_side_effects=True, vmem_limit_bytes=50 * 2**20
        ),
    )(
        *(
            pltpu.with_memory_space_constraint(a, pltpu.HBM)
            for a in (
                expert_ids.T, gate_weights.T, tokens, gate_proj[0], up_proj[0], down_proj[0]
            )
        )
    )


def solution(mesh):
    placed = (
        P("expert", "dp"),
        P("expert", None),
        P("expert", None),
        P("expert", "dp", None),
        P("expert", "dp", None),
        P("expert", None, "dp"),
    )
    return jax.shard_map(
        body, mesh=mesh, in_specs=placed, out_specs=P("expert", "dp"), check_vma=False
    )
```

```python
import functools

import jax
import jax.numpy as jnp
from jax import lax
from jax.experimental import pallas as pl
from jax.experimental.pallas import tpu as pltpu
from jax.sharding import PartitionSpec as P

MESH = pl.DeviceIdType.MESH
F32 = jnp.float32
BF16 = jnp.bfloat16


def quotient(a, b):
    return a // b if isinstance(a, int) else lax.div(a, jnp.int32(b))


def residue(a, b):
    return a % b if isinstance(a, int) else lax.rem(a, jnp.int32(b))


def z_shifts(n):
    order = sorted(range(n), key=lambda k: min(k, n - k))
    near, far = order[: n // 2], order[n // 2 :]
    return near[:1] + near[-1:] + near[1:-1], far[-1:] + far[:-1]


def iota(shape, dim):
    return lax.broadcasted_iota(jnp.int32, shape, dim)


def layer(
    n, per, ids_hbm, gw_hbm, tok_hbm, gate_hbm, up_hbm, down_hbm, out_ref,
    ids_ref, gw_ref, tok_ref, w_buf, d_buf, code_ref, mix_ref, packed, rows, parts, rs_out, rs_in, hid, outs, ret,
    load_sem, pack_send, pack_recv, rs_send, rs_recv, ag_send, ag_recv, ret_send, ret_recv,
):
    y = lax.axis_index("dp")
    me = lax.axis_index("expert")
    z, r = quotient(me, per), residue(me, per)
    x, c = quotient(r, 2), residue(r, 2)
    n_x, half, mid = per // 2, per // 2, n // 2
    experts = n * per
    top, toks = ids_ref.shape
    width = tok_ref.shape[1]
    cap = packed.shape[2]
    m_rows = half * cap
    ff = w_buf.shape[2]
    tile = min(ff, 512)
    sub_rows = m_rows // 2
    shifts = z_shifts(n)
    ahead, behind = residue(y + 1, n), residue(y + n - 1, n)
    steps = n - 1

    small = [
        pltpu.make_async_copy(ids_hbm, ids_ref, load_sem.at[3]),
        pltpu.make_async_copy(gw_hbm, gw_ref, load_sem.at[4]),
        pltpu.make_async_copy(tok_hbm, tok_ref, load_sem.at[5]),
    ]
    loads = [
        pltpu.make_async_copy(gate_hbm, w_buf.at[0], load_sem.at[0]),
        pltpu.make_async_copy(up_hbm, w_buf.at[1], load_sem.at[1]),
        pltpu.make_async_copy(down_hbm, d_buf, load_sem.at[2]),
    ]
    for load in small + loads:
        load.start()
    barrier = pltpu.get_barrier_semaphore()

    def greet(i, carry):
        pl.semaphore_signal(
            barrier, inc=1, device_id={"expert": residue(me + i, experts)}, device_id_type=MESH
        )
        return carry

    lax.fori_loop(1, experts, greet, 0)
    for to in (ahead, behind):
        pl.semaphore_signal(barrier, inc=1, device_id={"dp": to}, device_id_type=MESH)
    for load in small:
        load.wait()

    row = iota((experts, toks), 0)
    expert_of = row % n * per + row // n
    named = jnp.zeros((experts, toks), F32)
    picked = jnp.zeros((experts, toks), F32)
    for k in range(top):
        same = ids_ref[k : k + 1, :] == expert_of
        named = named + jnp.where(same, 1.0, 0.0)
        picked = picked + jnp.where(same, gw_ref[k : k + 1, :], 0.0)
    before = jnp.where(iota((toks, toks), 0) < iota((toks, toks), 1), 1.0, 0.0).astype(BF16)
    earlier = jnp.dot(named.astype(BF16), before, preferred_element_type=F32)
    code = jnp.where(named > 0.0, earlier, -1.0)
    code_ref[...] = code

    pl.semaphore_wait(barrier, experts - 1 + 2)

    def at_distance(i):
        k = mid - quotient(i + 1, 2)
        odd = residue(i, 2)
        return residue(y + odd * k + (1 - odd) * (n - k), n)

    def taker_of(p, j):
        dx = residue(quotient(p, 2) + j, n_x)
        return residue(x + n_x - dx, n_x) * 2 + residue(c + p, 2)

    def giver_of(p, j):
        dx = residue(quotient(p, 2) + j, n_x)
        return residue(x + dx, n_x) * 2 + residue(c + p, 2)

    def pack(h, i):
        p = at_distance(i)
        key = p * 2 + h
        takers = [(taker_of(p, j), residue(z + n - shift, n)) for j, shift in enumerate(shifts[h])]
        slot = iota((cap, toks), 0).astype(F32)
        chosen = jnp.concatenate(
            [
                jnp.where(code_ref[pl.ds(to_r * n + to_z, 1), :] == slot, 1.0, 0.0)
                for to_r, to_z in takers
            ],
            axis=0,
        )
        block = jnp.dot(chosen.astype(BF16), tok_ref[...], preferred_element_type=F32)
        packed[key] = block.astype(BF16).reshape(half, cap, width)
        for j, (to_r, to_z) in enumerate(takers):
            src, dst, sem = packed.at[key, j], rows.at[key, j], pack_recv.at[key]

            def remote():
                pltpu.make_async_remote_copy(
                    src_ref=src, dst_ref=dst, send_sem=pack_send, recv_sem=sem,
                    device_id={"expert": to_z * per + to_r}, device_id_type=MESH,
                ).start()

            if shifts[h][j] == 0:
                pl.when(p != 0)(remote)

                @pl.when(p == 0)
                def _():
                    pltpu.make_async_copy(src, dst, sem).start()

            else:
                remote()

    def pack_range(h, start, stop):
        def one(i, carry):
            pack(h, i)
            return carry

        lax.fori_loop(start, stop, one, 0)

    pack_range(0, 0, n // 2)
    for load in loads[:2]:
        load.wait()

    def await_rows(p, h):
        k = p * 2 + h
        pltpu.make_async_copy(rows.at[k], rows.at[k], pack_recv.at[k]).wait()

    def rows_of(p, h):
        return rows[p * 2 + h].reshape(m_rows, width)

    def send_sums(d, slot):
        pltpu.make_async_remote_copy(
            src_ref=rs_out.at[d, slot], dst_ref=rs_in.at[d, slot],
            send_sem=rs_send, recv_sem=rs_recv.at[d, slot],
            device_id={"dp": behind if d else ahead}, device_id_type=MESH,
        ).start()

    def reduce_step(h, i, joins):
        k = mid - quotient(i + 1, 2)
        if isinstance(i, int):
            await_rows(residue(y + k, n), h)
            if i:
                await_rows(residue(y + n - k, n), h)
        else:

            @pl.when(residue(i, 2) == 1)
            def _():
                await_rows(residue(y + k, n), h)
                await_rows(residue(y + n - k, n), h)

        slot = h * steps + i
        for d in (0, 1):
            own = rows_of(residue(y + (n - k if d else k), n), h)
            kind = residue(i + d, 2)
            for f in range(0, ff, tile):
                cut = slice(f, f + tile)
                part = jnp.dot(own, w_buf[kind, :, cut], preferred_element_type=F32)
                if joins:
                    parts[d, :, cut] = part
                else:
                    rs_out[d, slot, :, cut] = part.astype(BF16)
            if not joins:
                send_sums(d, slot)
        if joins:
            for d in (0, 1):
                came = rs_in.at[d, slot - 2]
                pltpu.make_async_copy(came, came, rs_recv.at[d, slot - 2]).wait()
                rs_out[d, slot] = (parts[d] + came[...].astype(F32)).astype(BF16)
                send_sums(d, slot)

    def make_mix():
        lane = iota((experts, experts * cap), 1)
        spread = jnp.where(lane // cap == iota((experts, experts * cap), 0), 1.0, 0.0).astype(BF16)
        slot_at = jnp.dot(code_ref[...].T.astype(BF16), spread, preferred_element_type=F32)
        here = slot_at == (iota((toks, experts * cap), 1) % cap).astype(F32)
        weights = picked.T
        high = weights.astype(BF16)
        low = (weights - high.astype(F32)).astype(BF16)
        for k, piece in enumerate((high, low)):
            laid = jnp.dot(piece, spread, preferred_element_type=F32)
            mix_ref[k * toks : (k + 1) * toks, :] = jnp.where(here, laid, 0.0).astype(BF16)

    def reduce_half(h):
        for i in range(2):
            reduce_step(h, i, False)
            if (h, i) == (0, 0):
                pack_range(0, n // 2, n)
        if h == 0:
            pack_range(1, 0, n // 2)
            loads[2].wait()

        def body(i, carry):
            reduce_step(h, i, True)
            if h == 0:

                @pl.when(i == 2)
                def _():
                    pack_range(1, n // 2, n)

            else:
                pl.when(i == (steps + 1) // 2)(begin_gather)
            return carry

        lax.fori_loop(2, steps, body, 0)

    def finish(h):
        await_rows(y, h)
        own = rows_of(y, h)
        for kind in (0, 1):
            for f in range(0, ff, tile):
                cut = slice(f, f + tile)
                parts[kind, :, cut] = jnp.dot(
                    own, w_buf[kind, :, cut], preferred_element_type=F32
                )
        last = h * steps + steps - 1
        for d in (0, 1):
            for slot in (last - 1, last):
                pltpu.make_async_copy(
                    rs_in.at[d, slot], rs_in.at[d, slot], rs_recv.at[d, slot]
                ).wait()
        for f in range(0, ff, tile):
            cut = slice(f, f + tile)
            gate = parts[0, :, cut] + rs_in[0, last, :, cut].astype(F32)
            gate = gate + rs_in[1, last - 1, :, cut].astype(F32)
            up = parts[1, :, cut] + rs_in[0, last - 1, :, cut].astype(F32)
            up = up + rs_in[1, last, :, cut].astype(F32)
            hid[h * n + y, :, cut] = (gate / (1.0 + jnp.exp(-gate)) * up).astype(BF16)

    def part_of(u, p, s, d):
        h, sub = divmod(u, 2)
        if s < mid - 1:
            return hid.at[h * n + p, pl.ds(sub * sub_rows, sub_rows)]
        few = sub_rows // 2
        return hid.at[h * n + p, pl.ds(sub * sub_rows + d * few, few)]

    def pass_on(u, s, d):
        part = part_of(u, residue(y + (s if d else n - s), n), s, d)
        pltpu.make_async_remote_copy(
            src_ref=part, dst_ref=part, send_sem=ag_send, recv_sem=ag_recv.at[d, u, s],
            device_id={"dp": behind if d else ahead}, device_id_type=MESH,
        ).start()

    def arrived(u, s, d):
        part = part_of(u, residue(y + (s + 1 if d else n - s - 1), n), s, d)
        pltpu.make_async_copy(part, part, ag_recv.at[d, u, s]).wait()

    def exchange(u, s):
        for d in (0, 1):
            if s > 0:
                arrived(u, s - 1, d)
            if s < mid:
                pass_on(u, s, d)

    def outward(u, s):
        h, sub = divmod(u, 2)
        pieces = [residue(y + s, n)]
        if 0 < s < mid:
            pieces.append(residue(y + n - s, n))
        keys = [h * n + p for p in pieces]
        cut = slice(sub * sub_rows, (sub + 1) * sub_rows)
        held = jnp.concatenate([hid[k, cut] for k in keys], axis=0)
        done = jnp.dot(held, d_buf[...], preferred_element_type=F32).astype(BF16)
        some = half // 2
        for i, (k, p) in enumerate(zip(keys, pieces)):
            block = done[i * sub_rows : (i + 1) * sub_rows]
            outs[k, sub * some : (sub + 1) * some] = block.reshape(some, cap, width)
            for j in range(sub * some, (sub + 1) * some):
                shift = shifts[h][j]
                src, dst = outs.at[k, j], ret.at[r * n + z]
                to = residue(z + shift, n) * per + giver_of(p, j)

                def remote():
                    pltpu.make_async_remote_copy(
                        src_ref=src, dst_ref=dst, send_sem=ret_send, recv_sem=ret_recv,
                        device_id={"expert": to}, device_id_type=MESH,
                    ).start()

                if shift == 0:
                    pl.when(p != 0)(remote)

                    @pl.when(p == 0)
                    def _():
                        pltpu.make_async_copy(src, dst, ret_recv).start()

                else:
                    remote()

    def begin_gather():
        finish(0)
        exchange(0, 0)
        outward(0, 0)

    reduce_half(0)
    make_mix()
    reduce_half(1)
    order = [
        (0, 1), (1, 0), (2, 0), (0, 2), (3, 0), (2, 1), (0, 3), (3, 1), (2, 2), (0, 4),
        (1, 1), (3, 2), (2, 3), (1, 2), (3, 3), (2, 4), (1, 3), (3, 4), (1, 4),
    ]
    late = None
    for u, s in order:
        if s > mid:
            continue
        if s == mid and late:
            outward(*late)
            late = None
        if (u, s) == (2, 0):
            finish(1)
        exchange(u, s)
        if late:
            outward(*late)
        late = (u, s)
    outward(*late)

    pltpu.make_async_copy(ret, ret, ret_recv).wait()
    back = ret[...].reshape(experts * cap, width)
    mixed = jnp.dot(mix_ref[...], back, preferred_element_type=F32)
    out_ref[...] = (mixed[:toks] + mixed[toks:]).astype(BF16)

    flat = packed.at[0, pl.ds(0, half - 1)]
    pltpu.make_async_copy(flat, flat, pack_send).wait()
    whole = packed.at[pl.ds(0, 2 * n - 1)]
    pltpu.make_async_copy(whole, whole, pack_send).wait()
    pltpu.make_async_copy(rs_out, rs_out, rs_send).wait()
    sent = hid.at[pl.ds(0, 2 * n - 2)]
    pltpu.make_async_copy(sent, sent, ag_send).wait()
    back_sent = ret.at[pl.ds(0, experts - 1)]
    pltpu.make_async_copy(back_sent, back_sent, ret_send).wait()


def body(tokens, expert_ids, gate_weights, gate_proj, up_proj, down_proj):
    n, experts = lax.axis_size("dp"), lax.axis_size("expert")
    per = experts // n
    assert per == n
    toks, width = tokens.shape
    top = expert_ids.shape[1]
    cap = 2 * toks * top // experts
    ff = gate_proj.shape[2]
    half = per // 2
    m_rows = half * cap
    vmem = pl.BlockSpec(memory_space=pltpu.VMEM)
    hbm = pl.BlockSpec(memory_space=pltpu.HBM)
    flops = 2 * experts * cap * width * ff * 3
    return pl.pallas_call(
        functools.partial(layer, n, per),
        out_shape=jax.ShapeDtypeStruct((toks, width), BF16),
        in_specs=[hbm] * 6,
        out_specs=vmem,
        scratch_shapes=[
            pltpu.VMEM((top, toks), jnp.int32),
            pltpu.VMEM((top, toks), F32),
            pltpu.VMEM((toks, width), BF16),
            pltpu.VMEM((2, width, ff), BF16),
            pltpu.VMEM((ff, width), BF16),
            pltpu.VMEM((experts, toks), F32),
            pltpu.VMEM((2 * toks, experts * cap), BF16),
            pltpu.VMEM((2 * n, half, cap, width), BF16),
            pltpu.VMEM((2 * n, half, cap, width), BF16),
            pltpu.VMEM((2, m_rows, ff), F32),
            pltpu.VMEM((2, 2 * (n - 1), m_rows, ff), BF16),
            pltpu.VMEM((2, 2 * (n - 1), m_rows, ff), BF16),
            pltpu.VMEM((2 * n, m_rows, ff), BF16),
            pltpu.VMEM((2 * n, half, cap, width), BF16),
            pltpu.VMEM((experts, cap, width), BF16),
            pltpu.SemaphoreType.DMA((6,)),
            pltpu.SemaphoreType.DMA,
            pltpu.SemaphoreType.DMA((2 * n,)),
            pltpu.SemaphoreType.DMA,
            pltpu.SemaphoreType.DMA((2, 2 * (n - 1))),
            pltpu.SemaphoreType.DMA,
            pltpu.SemaphoreType.DMA((2, 4, n // 2)),
            pltpu.SemaphoreType.DMA,
            pltpu.SemaphoreType.DMA,
        ],
        cost_estimate=pl.CostEstimate(
            flops=flops, bytes_accessed=3 * width * ff * 2, transcendentals=m_rows * 2 * ff
        ),
        compiler_params=pltpu.CompilerParams(
            collective_id=0, has_side_effects=True, vmem_limit_bytes=50 * 2**20
        ),
    )(
        *(
            pltpu.with_memory_space_constraint(a, pltpu.HBM)
            for a in (
                expert_ids.T, gate_weights.T, tokens, gate_proj[0], up_proj[0], down_proj[0]
            )
        )
    )


def solution(mesh):
    placed = (
        P("expert", "dp"),
        P("expert", None),
        P("expert", None),
        P("expert", "dp", None),
        P("expert", "dp", None),
        P("expert", None, "dp"),
    )
    return jax.shard_map(
        body, mesh=mesh, in_specs=placed, out_specs=P("expert", "dp"), check_vma=False
    )
```

```python
import functools

import jax
import jax.numpy as jnp
from jax import lax
from jax.experimental import pallas as pl
from jax.experimental.pallas import tpu as pltpu
from jax.sharding import PartitionSpec as P

MESH = pl.DeviceIdType.MESH
F32 = jnp.float32
BF16 = jnp.bfloat16


def quotient(a, b):
    return a // b if isinstance(a, int) else lax.div(a, jnp.int32(b))


def residue(a, b):
    return a % b if isinstance(a, int) else lax.rem(a, jnp.int32(b))


def z_shifts(n):
    order = sorted(range(n), key=lambda k: min(k, n - k))
    near, far = order[: n // 2], order[n // 2 :]
    return near[:1] + near[-1:] + near[1:-1], far[-1:] + far[:-1]


def iota(shape, dim):
    return lax.broadcasted_iota(jnp.int32, shape, dim)


def layer(
    n, per, ids_hbm, gw_hbm, tok_hbm, gate_hbm, up_hbm, down_hbm, out_ref,
    ids_ref, gw_ref, tok_ref, w_buf, d_buf, code_ref, mix_ref, packed, rows, parts, rs_out, rs_in, hid, outs, ret,
    load_sem, pack_send, pack_recv, rs_send, rs_recv, ag_send, ag_recv, ret_send, ret_recv,
):
    y = lax.axis_index("dp")
    me = lax.axis_index("expert")
    z, r = quotient(me, per), residue(me, per)
    x, c = quotient(r, 2), residue(r, 2)
    n_x, half, mid = per // 2, per // 2, n // 2
    experts = n * per
    top, toks = ids_ref.shape
    width = tok_ref.shape[1]
    cap = packed.shape[2]
    m_rows = half * cap
    ff = w_buf.shape[2]
    tile = min(ff, 512)
    sub_rows = m_rows // 2
    shifts = z_shifts(n)
    ahead, behind = residue(y + 1, n), residue(y + n - 1, n)
    steps = n - 1

    small = [
        pltpu.make_async_copy(ids_hbm, ids_ref, load_sem.at[3]),
        pltpu.make_async_copy(gw_hbm, gw_ref, load_sem.at[4]),
        pltpu.make_async_copy(tok_hbm, tok_ref, load_sem.at[5]),
    ]
    loads = [
        pltpu.make_async_copy(gate_hbm, w_buf.at[0], load_sem.at[0]),
        pltpu.make_async_copy(up_hbm, w_buf.at[1], load_sem.at[1]),
        pltpu.make_async_copy(down_hbm, d_buf, load_sem.at[2]),
    ]
    for load in small + loads:
        load.start()
    barrier = pltpu.get_barrier_semaphore()

    def greet(i, carry):
        pl.semaphore_signal(
            barrier, inc=1, device_id={"expert": residue(me + i, experts)}, device_id_type=MESH
        )
        return carry

    lax.fori_loop(1, experts, greet, 0)
    for to in (ahead, behind):
        pl.semaphore_signal(barrier, inc=1, device_id={"dp": to}, device_id_type=MESH)
    for load in small:
        load.wait()

    row = iota((experts, toks), 0)
    expert_of = row % n * per + row // n
    named = jnp.zeros((experts, toks), F32)
    picked = jnp.zeros((experts, toks), F32)
    for k in range(top):
        same = ids_ref[k : k + 1, :] == expert_of
        named = named + jnp.where(same, 1.0, 0.0)
        picked = picked + jnp.where(same, gw_ref[k : k + 1, :], 0.0)
    before = jnp.where(iota((toks, toks), 0) < iota((toks, toks), 1), 1.0, 0.0).astype(BF16)
    earlier = jnp.dot(named.astype(BF16), before, preferred_element_type=F32)
    code = jnp.where(named > 0.0, earlier, -1.0)
    code_ref[...] = code

    pl.semaphore_wait(barrier, experts - 1 + 2)

    def at_distance(i):
        k = mid - quotient(i + 1, 2)
        odd = residue(i, 2)
        return residue(y + odd * k + (1 - odd) * (n - k), n)

    def taker_of(p, j):
        dx = residue(quotient(p, 2) + j, n_x)
        return residue(x + n_x - dx, n_x) * 2 + residue(c + p, 2)

    def giver_of(p, j):
        dx = residue(quotient(p, 2) + j, n_x)
        return residue(x + dx, n_x) * 2 + residue(c + p, 2)

    def pack(h, i):
        p = at_distance(i)
        key = p * 2 + h
        takers = [(taker_of(p, j), residue(z + n - shift, n)) for j, shift in enumerate(shifts[h])]
        slot = iota((cap, toks), 0).astype(F32)
        chosen = jnp.concatenate(
            [
                jnp.where(code_ref[pl.ds(to_r * n + to_z, 1), :] == slot, 1.0, 0.0)
                for to_r, to_z in takers
            ],
            axis=0,
        )
        block = jnp.dot(chosen.astype(BF16), tok_ref[...], preferred_element_type=F32)
        packed[key] = block.astype(BF16).reshape(half, cap, width)
        for j, (to_r, to_z) in enumerate(takers):
            src, dst, sem = packed.at[key, j], rows.at[key, j], pack_recv.at[key]

            def remote():
                pltpu.make_async_remote_copy(
                    src_ref=src, dst_ref=dst, send_sem=pack_send, recv_sem=sem,
                    device_id={"expert": to_z * per + to_r}, device_id_type=MESH,
                ).start()

            if shifts[h][j] == 0:
                pl.when(p != 0)(remote)

                @pl.when(p == 0)
                def _():
                    pltpu.make_async_copy(src, dst, sem).start()

            else:
                remote()

    def pack_range(h, start, stop):
        def one(i, carry):
            pack(h, i)
            return carry

        lax.fori_loop(start, stop, one, 0)

    pack_range(0, 0, n // 2)
    for load in loads[:2]:
        load.wait()

    def await_rows(p, h):
        k = p * 2 + h
        pltpu.make_async_copy(rows.at[k], rows.at[k], pack_recv.at[k]).wait()

    def rows_of(p, h):
        return rows[p * 2 + h].reshape(m_rows, width)

    def send_sums(d, slot):
        pltpu.make_async_remote_copy(
            src_ref=rs_out.at[d, slot], dst_ref=rs_in.at[d, slot],
            send_sem=rs_send, recv_sem=rs_recv.at[d, slot],
            device_id={"dp": behind if d else ahead}, device_id_type=MESH,
        ).start()

    def reduce_step(h, i, joins):
        k = mid - quotient(i + 1, 2)
        if isinstance(i, int):
            await_rows(residue(y + k, n), h)
            if i:
                await_rows(residue(y + n - k, n), h)
        else:

            @pl.when(residue(i, 2) == 1)
            def _():
                await_rows(residue(y + k, n), h)
                await_rows(residue(y + n - k, n), h)

        slot = h * steps + i
        for d in (0, 1):
            own = rows_of(residue(y + (n - k if d else k), n), h)
            kind = residue(i + d, 2)
            for f in range(0, ff, tile):
                cut = slice(f, f + tile)
                part = jnp.dot(own, w_buf[kind, :, cut], preferred_element_type=F32)
                if joins:
                    parts[d, :, cut] = part
                else:
                    rs_out[d, slot, :, cut] = part.astype(BF16)
            if not joins:
                send_sums(d, slot)
        if joins:
            for d in (0, 1):
                came = rs_in.at[d, slot - 2]
                pltpu.make_async_copy(came, came, rs_recv.at[d, slot - 2]).wait()
                rs_out[d, slot] = (parts[d] + came[...].astype(F32)).astype(BF16)
                send_sums(d, slot)

    def make_mix():
        lane = iota((experts, experts * cap), 1)
        spread = jnp.where(lane // cap == iota((experts, experts * cap), 0), 1.0, 0.0).astype(BF16)
        slot_at = jnp.dot(code_ref[...].T.astype(BF16), spread, preferred_element_type=F32)
        here = slot_at == (iota((toks, experts * cap), 1) % cap).astype(F32)
        weights = picked.T
        high = weights.astype(BF16)
        low = (weights - high.astype(F32)).astype(BF16)
        for k, piece in enumerate((high, low)):
            laid = jnp.dot(piece, spread, preferred_element_type=F32)
            mix_ref[k * toks : (k + 1) * toks, :] = jnp.where(here, laid, 0.0).astype(BF16)

    def reduce_half(h):
        for i in range(2):
            reduce_step(h, i, False)
            if (h, i) == (0, 0):
                pack_range(0, n // 2, n)
        if h == 0:
            pack_range(1, 0, n // 2)
            loads[2].wait()

        def body(i, carry):
            reduce_step(h, i, True)
            if h == 0:

                @pl.when(i == 2)
                def _():
                    pack_range(1, n // 2, n)

            else:
                pl.when(i == (steps + 1) // 2)(begin_gather)
            return carry

        lax.fori_loop(2, steps, body, 0)

    def finish(h):
        await_rows(y, h)
        own = rows_of(y, h)
        for kind in (0, 1):
            for f in range(0, ff, tile):
                cut = slice(f, f + tile)
                parts[kind, :, cut] = jnp.dot(
                    own, w_buf[kind, :, cut], preferred_element_type=F32
                )
        last = h * steps + steps - 1
        for d in (0, 1):
            for slot in (last - 1, last):
                pltpu.make_async_copy(
                    rs_in.at[d, slot], rs_in.at[d, slot], rs_recv.at[d, slot]
                ).wait()
        for f in range(0, ff, tile):
            cut = slice(f, f + tile)
            gate = parts[0, :, cut] + rs_in[0, last, :, cut].astype(F32)
            gate = gate + rs_in[1, last - 1, :, cut].astype(F32)
            up = parts[1, :, cut] + rs_in[0, last - 1, :, cut].astype(F32)
            up = up + rs_in[1, last, :, cut].astype(F32)
            hid[h * n + y, :, cut] = (gate / (1.0 + jnp.exp(-gate)) * up).astype(BF16)

    def part_of(u, p, s, d):
        h, sub = divmod(u, 2)
        if s < mid - 1:
            return hid.at[h * n + p, pl.ds(sub * sub_rows, sub_rows)]
        few = sub_rows // 2
        return hid.at[h * n + p, pl.ds(sub * sub_rows + d * few, few)]

    def pass_on(u, s, d):
        part = part_of(u, residue(y + (s if d else n - s), n), s, d)
        pltpu.make_async_remote_copy(
            src_ref=part, dst_ref=part, send_sem=ag_send, recv_sem=ag_recv.at[d, u, s],
            device_id={"dp": behind if d else ahead}, device_id_type=MESH,
        ).start()

    def arrived(u, s, d):
        part = part_of(u, residue(y + (s + 1 if d else n - s - 1), n), s, d)
        pltpu.make_async_copy(part, part, ag_recv.at[d, u, s]).wait()

    def exchange(u, s):
        for d in (0, 1):
            if s > 0:
                arrived(u, s - 1, d)
            if s < mid:
                pass_on(u, s, d)

    def outward(u, s):
        h, sub = divmod(u, 2)
        pieces = [residue(y + s, n)]
        if 0 < s < mid:
            pieces.append(residue(y + n - s, n))
        keys = [h * n + p for p in pieces]
        cut = slice(sub * sub_rows, (sub + 1) * sub_rows)
        held = jnp.concatenate([hid[k, cut] for k in keys], axis=0)
        done = jnp.dot(held, d_buf[...], preferred_element_type=F32).astype(BF16)
        some = half // 2
        for i, (k, p) in enumerate(zip(keys, pieces)):
            block = done[i * sub_rows : (i + 1) * sub_rows]
            outs[k, sub * some : (sub + 1) * some] = block.reshape(some, cap, width)
            for j in range(sub * some, (sub + 1) * some):
                shift = shifts[h][j]
                src, dst = outs.at[k, j], ret.at[r * n + z]
                to = residue(z + shift, n) * per + giver_of(p, j)

                def remote():
                    pltpu.make_async_remote_copy(
                        src_ref=src, dst_ref=dst, send_sem=ret_send, recv_sem=ret_recv,
                        device_id={"expert": to}, device_id_type=MESH,
                    ).start()

                if shift == 0:
                    pl.when(p != 0)(remote)

                    @pl.when(p == 0)
                    def _():
                        pltpu.make_async_copy(src, dst, ret_recv).start()

                else:
                    remote()

    def begin_gather():
        finish(0)
        exchange(0, 0)
        outward(0, 0)

    reduce_half(0)
    make_mix()
    reduce_half(1)
    order = [
        (0, 1), (1, 0), (2, 0), (3, 0), (0, 2), (2, 1), (3, 1), (0, 3), (2, 2), (1, 1),
        (3, 2), (1, 2), (2, 3), (0, 4), (3, 3), (1, 3), (2, 4), (3, 4), (1, 4),
    ]
    late = None
    for u, s in order:
        if s > mid:
            continue
        if s == mid and late:
            outward(*late)
            late = None
        if (u, s) == (2, 0):
            finish(1)
        exchange(u, s)
        if late:
            outward(*late)
        late = (u, s)
    outward(*late)

    pltpu.make_async_copy(ret, ret, ret_recv).wait()
    back = ret[...].reshape(experts * cap, width)
    mixed = jnp.dot(mix_ref[...], back, preferred_element_type=F32)
    out_ref[...] = (mixed[:toks] + mixed[toks:]).astype(BF16)

    flat = packed.at[0, pl.ds(0, half - 1)]
    pltpu.make_async_copy(flat, flat, pack_send).wait()
    whole = packed.at[pl.ds(0, 2 * n - 1)]
    pltpu.make_async_copy(whole, whole, pack_send).wait()
    pltpu.make_async_copy(rs_out, rs_out, rs_send).wait()
    sent = hid.at[pl.ds(0, 2 * n - 2)]
    pltpu.make_async_copy(sent, sent, ag_send).wait()
    back_sent = ret.at[pl.ds(0, experts - 1)]
    pltpu.make_async_copy(back_sent, back_sent, ret_send).wait()


def body(tokens, expert_ids, gate_weights, gate_proj, up_proj, down_proj):
    n, experts = lax.axis_size("dp"), lax.axis_size("expert")
    per = experts // n
    assert per == n
    toks, width = tokens.shape
    top = expert_ids.shape[1]
    cap = 2 * toks * top // experts
    ff = gate_proj.shape[2]
    half = per // 2
    m_rows = half * cap
    vmem = pl.BlockSpec(memory_space=pltpu.VMEM)
    hbm = pl.BlockSpec(memory_space=pltpu.HBM)
    flops = 2 * experts * cap * width * ff * 3
    return pl.pallas_call(
        functools.partial(layer, n, per),
        out_shape=jax.ShapeDtypeStruct((toks, width), BF16),
        in_specs=[hbm] * 6,
        out_specs=vmem,
        scratch_shapes=[
            pltpu.VMEM((top, toks), jnp.int32),
            pltpu.VMEM((top, toks), F32),
            pltpu.VMEM((toks, width), BF16),
            pltpu.VMEM((2, width, ff), BF16),
            pltpu.VMEM((ff, width), BF16),
            pltpu.VMEM((experts, toks), F32),
            pltpu.VMEM((2 * toks, experts * cap), BF16),
            pltpu.VMEM((2 * n, half, cap, width), BF16),
            pltpu.VMEM((2 * n, half, cap, width), BF16),
            pltpu.VMEM((2, m_rows, ff), F32),
            pltpu.VMEM((2, 2 * (n - 1), m_rows, ff), BF16),
            pltpu.VMEM((2, 2 * (n - 1), m_rows, ff), BF16),
            pltpu.VMEM((2 * n, m_rows, ff), BF16),
            pltpu.VMEM((2 * n, half, cap, width), BF16),
            pltpu.VMEM((experts, cap, width), BF16),
            pltpu.SemaphoreType.DMA((6,)),
            pltpu.SemaphoreType.DMA,
            pltpu.SemaphoreType.DMA((2 * n,)),
            pltpu.SemaphoreType.DMA,
            pltpu.SemaphoreType.DMA((2, 2 * (n - 1))),
            pltpu.SemaphoreType.DMA,
            pltpu.SemaphoreType.DMA((2, 4, n // 2)),
            pltpu.SemaphoreType.DMA,
            pltpu.SemaphoreType.DMA,
        ],
        cost_estimate=pl.CostEstimate(
            flops=flops, bytes_accessed=3 * width * ff * 2, transcendentals=m_rows * 2 * ff
        ),
        compiler_params=pltpu.CompilerParams(
            collective_id=0, has_side_effects=True, vmem_limit_bytes=50 * 2**20
        ),
    )(
        *(
            pltpu.with_memory_space_constraint(a, pltpu.HBM)
            for a in (
                expert_ids.T, gate_weights.T, tokens, gate_proj[0], up_proj[0], down_proj[0]
            )
        )
    )


def solution(mesh):
    placed = (
        P("expert", "dp"),
        P("expert", None),
        P("expert", None),
        P("expert", "dp", None),
        P("expert", "dp", None),
        P("expert", None, "dp"),
    )
    return jax.shard_map(
        body, mesh=mesh, in_specs=placed, out_specs=P("expert", "dp"), check_vma=False
    )
```

```python
import functools

import jax
import jax.numpy as jnp
from jax import lax
from jax.experimental import pallas as pl
from jax.experimental.pallas import tpu as pltpu
from jax.sharding import PartitionSpec as P

MESH = pl.DeviceIdType.MESH
F32 = jnp.float32
BF16 = jnp.bfloat16


def quotient(a, b):
    return a // b if isinstance(a, int) else lax.div(a, jnp.int32(b))


def residue(a, b):
    return a % b if isinstance(a, int) else lax.rem(a, jnp.int32(b))


def z_shifts(n):
    order = sorted(range(n), key=lambda k: min(k, n - k))
    near, far = order[: n // 2], order[n // 2 :]
    return near[:1] + near[-1:] + near[1:-1], far[-1:] + far[:-1]


def iota(shape, dim):
    return lax.broadcasted_iota(jnp.int32, shape, dim)


def layer(
    n, per, ids_hbm, gw_hbm, tok_hbm, gate_hbm, up_hbm, down_hbm, out_ref,
    ids_ref, gw_ref, tok_ref, w_buf, d_buf, code_ref, mix_ref, packed, rows, parts, rs_out, rs_in, hid, outs, ret,
    load_sem, pack_send, pack_recv, rs_send, rs_recv, ag_send, ag_recv, ret_send, ret_recv,
):
    y = lax.axis_index("dp")
    me = lax.axis_index("expert")
    z, r = quotient(me, per), residue(me, per)
    x, c = quotient(r, 2), residue(r, 2)
    n_x, half, mid = per // 2, per // 2, n // 2
    experts = n * per
    top, toks = ids_ref.shape
    width = tok_ref.shape[1]
    cap = packed.shape[2]
    m_rows = half * cap
    ff = w_buf.shape[2]
    tile = min(ff, 512)
    sub_rows = m_rows // 2
    shifts = z_shifts(n)
    ahead, behind = residue(y + 1, n), residue(y + n - 1, n)
    steps = n - 1

    small = [
        pltpu.make_async_copy(ids_hbm, ids_ref, load_sem.at[3]),
        pltpu.make_async_copy(gw_hbm, gw_ref, load_sem.at[4]),
        pltpu.make_async_copy(tok_hbm, tok_ref, load_sem.at[5]),
    ]
    loads = [
        pltpu.make_async_copy(gate_hbm, w_buf.at[0], load_sem.at[0]),
        pltpu.make_async_copy(up_hbm, w_buf.at[1], load_sem.at[1]),
        pltpu.make_async_copy(down_hbm, d_buf, load_sem.at[2]),
    ]
    for load in small + loads:
        load.start()
    barrier = pltpu.get_barrier_semaphore()

    def greet(i, carry):
        pl.semaphore_signal(
            barrier, inc=1, device_id={"expert": residue(me + i, experts)}, device_id_type=MESH
        )
        return carry

    lax.fori_loop(1, experts, greet, 0)
    for to in (ahead, behind):
        pl.semaphore_signal(barrier, inc=1, device_id={"dp": to}, device_id_type=MESH)
    for load in small:
        load.wait()

    row = iota((experts, toks), 0)
    expert_of = row % n * per + row // n
    named = jnp.zeros((experts, toks), F32)
    picked = jnp.zeros((experts, toks), F32)
    for k in range(top):
        same = ids_ref[k : k + 1, :] == expert_of
        named = named + jnp.where(same, 1.0, 0.0)
        picked = picked + jnp.where(same, gw_ref[k : k + 1, :], 0.0)
    before = jnp.where(iota((toks, toks), 0) < iota((toks, toks), 1), 1.0, 0.0).astype(BF16)
    earlier = jnp.dot(named.astype(BF16), before, preferred_element_type=F32)
    code = jnp.where(named > 0.0, earlier, -1.0)
    code_ref[...] = code

    pl.semaphore_wait(barrier, experts - 1 + 2)

    def at_distance(i):
        k = mid - quotient(i + 1, 2)
        odd = residue(i, 2)
        return residue(y + odd * k + (1 - odd) * (n - k), n)

    def taker_of(p, j):
        dx = residue(quotient(p, 2) + j, n_x)
        return residue(x + n_x - dx, n_x) * 2 + residue(c + p, 2)

    def giver_of(p, j):
        dx = residue(quotient(p, 2) + j, n_x)
        return residue(x + dx, n_x) * 2 + residue(c + p, 2)

    def pack(h, i):
        p = at_distance(i)
        key = p * 2 + h
        takers = [(taker_of(p, j), residue(z + n - shift, n)) for j, shift in enumerate(shifts[h])]
        slot = iota((cap, toks), 0).astype(F32)
        chosen = jnp.concatenate(
            [
                jnp.where(code_ref[pl.ds(to_r * n + to_z, 1), :] == slot, 1.0, 0.0)
                for to_r, to_z in takers
            ],
            axis=0,
        )
        block = jnp.dot(chosen.astype(BF16), tok_ref[...], preferred_element_type=F32)
        packed[key] = block.astype(BF16).reshape(half, cap, width)
        for j, (to_r, to_z) in enumerate(takers):
            src, dst, sem = packed.at[key, j], rows.at[key, j], pack_recv.at[key]

            def remote():
                pltpu.make_async_remote_copy(
                    src_ref=src, dst_ref=dst, send_sem=pack_send, recv_sem=sem,
                    device_id={"expert": to_z * per + to_r}, device_id_type=MESH,
                ).start()

            if shifts[h][j] == 0:
                pl.when(p != 0)(remote)

                @pl.when(p == 0)
                def _():
                    pltpu.make_async_copy(src, dst, sem).start()

            else:
                remote()

    def pack_range(h, start, stop):
        def one(i, carry):
            pack(h, i)
            return carry

        lax.fori_loop(start, stop, one, 0)

    pack_range(0, 0, n // 2 - 1)
    for load in loads[:2]:
        load.wait()

    def await_rows(p, h):
        k = p * 2 + h
        pltpu.make_async_copy(rows.at[k], rows.at[k], pack_recv.at[k]).wait()

    def rows_of(p, h):
        return rows[p * 2 + h].reshape(m_rows, width)

    def send_sums(d, slot):
        pltpu.make_async_remote_copy(
            src_ref=rs_out.at[d, slot], dst_ref=rs_in.at[d, slot],
            send_sem=rs_send, recv_sem=rs_recv.at[d, slot],
            device_id={"dp": behind if d else ahead}, device_id_type=MESH,
        ).start()

    def reduce_step(h, i, joins):
        k = mid - quotient(i + 1, 2)
        if isinstance(i, int):
            await_rows(residue(y + k, n), h)
            if i:
                await_rows(residue(y + n - k, n), h)
        else:

            @pl.when(residue(i, 2) == 1)
            def _():
                await_rows(residue(y + k, n), h)
                await_rows(residue(y + n - k, n), h)

        slot = h * steps + i
        for d in (0, 1):
            own = rows_of(residue(y + (n - k if d else k), n), h)
            kind = residue(i + d, 2)
            for f in range(0, ff, tile):
                cut = slice(f, f + tile)
                part = jnp.dot(own, w_buf[kind, :, cut], preferred_element_type=F32)
                if joins:
                    parts[d, :, cut] = part
                else:
                    rs_out[d, slot, :, cut] = part.astype(BF16)
            if not joins:
                send_sums(d, slot)
        if joins:
            for d in (0, 1):
                came = rs_in.at[d, slot - 2]
                pltpu.make_async_copy(came, came, rs_recv.at[d, slot - 2]).wait()
                rs_out[d, slot] = (parts[d] + came[...].astype(F32)).astype(BF16)
                send_sums(d, slot)

    def make_mix():
        lane = iota((experts, experts * cap), 1)
        spread = jnp.where(lane // cap == iota((experts, experts * cap), 0), 1.0, 0.0).astype(BF16)
        slot_at = jnp.dot(code_ref[...].T.astype(BF16), spread, preferred_element_type=F32)
        here = slot_at == (iota((toks, experts * cap), 1) % cap).astype(F32)
        weights = picked.T
        high = weights.astype(BF16)
        low = (weights - high.astype(F32)).astype(BF16)
        for k, piece in enumerate((high, low)):
            laid = jnp.dot(piece, spread, preferred_element_type=F32)
            mix_ref[k * toks : (k + 1) * toks, :] = jnp.where(here, laid, 0.0).astype(BF16)

    def reduce_half(h):
        for i in range(2):
            reduce_step(h, i, False)
            if (h, i) == (0, 0):
                pack_range(0, n // 2 - 1, n)
        if h == 0:
            pack_range(1, 0, n // 2)
            loads[2].wait()

        def body(i, carry):
            reduce_step(h, i, True)
            if h == 0:

                @pl.when(i == 2)
                def _():
                    pack_range(1, n // 2, n)

            else:
                pl.when(i == (steps + 1) // 2)(begin_gather)
            return carry

        lax.fori_loop(2, steps, body, 0)

    def finish(h):
        await_rows(y, h)
        own = rows_of(y, h)
        for kind in (0, 1):
            for f in range(0, ff, tile):
                cut = slice(f, f + tile)
                parts[kind, :, cut] = jnp.dot(
                    own, w_buf[kind, :, cut], preferred_element_type=F32
                )
        last = h * steps + steps - 1
        for d in (0, 1):
            for slot in (last - 1, last):
                pltpu.make_async_copy(
                    rs_in.at[d, slot], rs_in.at[d, slot], rs_recv.at[d, slot]
                ).wait()
        for f in range(0, ff, tile):
            cut = slice(f, f + tile)
            gate = parts[0, :, cut] + rs_in[0, last, :, cut].astype(F32)
            gate = gate + rs_in[1, last - 1, :, cut].astype(F32)
            up = parts[1, :, cut] + rs_in[0, last - 1, :, cut].astype(F32)
            up = up + rs_in[1, last, :, cut].astype(F32)
            hid[h * n + y, :, cut] = (gate / (1.0 + jnp.exp(-gate)) * up).astype(BF16)

    def part_of(u, p, s, d):
        h, sub = divmod(u, 2)
        if s < mid - 1:
            return hid.at[h * n + p, pl.ds(sub * sub_rows, sub_rows)]
        few = sub_rows // 2
        return hid.at[h * n + p, pl.ds(sub * sub_rows + d * few, few)]

    def pass_on(u, s, d):
        part = part_of(u, residue(y + (s if d else n - s), n), s, d)
        pltpu.make_async_remote_copy(
            src_ref=part, dst_ref=part, send_sem=ag_send, recv_sem=ag_recv.at[d, u, s],
            device_id={"dp": behind if d else ahead}, device_id_type=MESH,
        ).start()

    def arrived(u, s, d):
        part = part_of(u, residue(y + (s + 1 if d else n - s - 1), n), s, d)
        pltpu.make_async_copy(part, part, ag_recv.at[d, u, s]).wait()

    def exchange(u, s):
        for d in (0, 1):
            if s > 0:
                arrived(u, s - 1, d)
            if s < mid:
                pass_on(u, s, d)

    def outward(u, s):
        h, sub = divmod(u, 2)
        pieces = [residue(y + s, n)]
        if 0 < s < mid:
            pieces.append(residue(y + n - s, n))
        keys = [h * n + p for p in pieces]
        cut = slice(sub * sub_rows, (sub + 1) * sub_rows)
        held = jnp.concatenate([hid[k, cut] for k in keys], axis=0)
        done = jnp.dot(held, d_buf[...], preferred_element_type=F32).astype(BF16)
        some = half // 2
        for i, (k, p) in enumerate(zip(keys, pieces)):
            block = done[i * sub_rows : (i + 1) * sub_rows]
            outs[k, sub * some : (sub + 1) * some] = block.reshape(some, cap, width)
            for j in range(sub * some, (sub + 1) * some):
                shift = shifts[h][j]
                src, dst = outs.at[k, j], ret.at[r * n + z]
                to = residue(z + shift, n) * per + giver_of(p, j)

                def remote():
                    pltpu.make_async_remote_copy(
                        src_ref=src, dst_ref=dst, send_sem=ret_send, recv_sem=ret_recv,
                        device_id={"expert": to}, device_id_type=MESH,
                    ).start()

                if shift == 0:
                    pl.when(p != 0)(remote)

                    @pl.when(p == 0)
                    def _():
                        pltpu.make_async_copy(src, dst, ret_recv).start()

                else:
                    remote()

    def begin_gather():
        finish(0)
        exchange(0, 0)
        outward(0, 0)

    reduce_half(0)
    make_mix()
    reduce_half(1)
    order = [
        (0, 1), (1, 0), (2, 0), (0, 2), (3, 0), (2, 1), (0, 3), (3, 1), (2, 2), (0, 4),
        (1, 1), (3, 2), (2, 3), (1, 2), (3, 3), (1, 3), (2, 4), (3, 4), (1, 4),
    ]
    late = None
    for u, s in order:
        if s > mid:
            continue
        if s == mid and late:
            outward(*late)
            late = None
        if (u, s) == (2, 0):
            finish(1)
        exchange(u, s)
        if late:
            outward(*late)
        late = (u, s)
    outward(*late)

    pltpu.make_async_copy(ret, ret, ret_recv).wait()
    back = ret[...].reshape(experts * cap, width)
    mixed = jnp.dot(mix_ref[...], back, preferred_element_type=F32)
    out_ref[...] = (mixed[:toks] + mixed[toks:]).astype(BF16)

    flat = packed.at[0, pl.ds(0, half - 1)]
    pltpu.make_async_copy(flat, flat, pack_send).wait()
    whole = packed.at[pl.ds(0, 2 * n - 1)]
    pltpu.make_async_copy(whole, whole, pack_send).wait()
    pltpu.make_async_copy(rs_out, rs_out, rs_send).wait()
    sent = hid.at[pl.ds(0, 2 * n - 2)]
    pltpu.make_async_copy(sent, sent, ag_send).wait()
    back_sent = ret.at[pl.ds(0, experts - 1)]
    pltpu.make_async_copy(back_sent, back_sent, ret_send).wait()


def body(tokens, expert_ids, gate_weights, gate_proj, up_proj, down_proj):
    n, experts = lax.axis_size("dp"), lax.axis_size("expert")
    per = experts // n
    assert per == n
    toks, width = tokens.shape
    top = expert_ids.shape[1]
    cap = 2 * toks * top // experts
    ff = gate_proj.shape[2]
    half = per // 2
    m_rows = half * cap
    vmem = pl.BlockSpec(memory_space=pltpu.VMEM)
    hbm = pl.BlockSpec(memory_space=pltpu.HBM)
    flops = 2 * experts * cap * width * ff * 3
    return pl.pallas_call(
        functools.partial(layer, n, per),
        out_shape=jax.ShapeDtypeStruct((toks, width), BF16),
        in_specs=[hbm] * 6,
        out_specs=vmem,
        scratch_shapes=[
            pltpu.VMEM((top, toks), jnp.int32),
            pltpu.VMEM((top, toks), F32),
            pltpu.VMEM((toks, width), BF16),
            pltpu.VMEM((2, width, ff), BF16),
            pltpu.VMEM((ff, width), BF16),
            pltpu.VMEM((experts, toks), F32),
            pltpu.VMEM((2 * toks, experts * cap), BF16),
            pltpu.VMEM((2 * n, half, cap, width), BF16),
            pltpu.VMEM((2 * n, half, cap, width), BF16),
            pltpu.VMEM((2, m_rows, ff), F32),
            pltpu.VMEM((2, 2 * (n - 1), m_rows, ff), BF16),
            pltpu.VMEM((2, 2 * (n - 1), m_rows, ff), BF16),
            pltpu.VMEM((2 * n, m_rows, ff), BF16),
            pltpu.VMEM((2 * n, half, cap, width), BF16),
            pltpu.VMEM((experts, cap, width), BF16),
            pltpu.SemaphoreType.DMA((6,)),
            pltpu.SemaphoreType.DMA,
            pltpu.SemaphoreType.DMA((2 * n,)),
            pltpu.SemaphoreType.DMA,
            pltpu.SemaphoreType.DMA((2, 2 * (n - 1))),
            pltpu.SemaphoreType.DMA,
            pltpu.SemaphoreType.DMA((2, 4, n // 2)),
            pltpu.SemaphoreType.DMA,
            pltpu.SemaphoreType.DMA,
        ],
        cost_estimate=pl.CostEstimate(
            flops=flops, bytes_accessed=3 * width * ff * 2, transcendentals=m_rows * 2 * ff
        ),
        compiler_params=pltpu.CompilerParams(
            collective_id=0, has_side_effects=True, vmem_limit_bytes=50 * 2**20
        ),
    )(
        *(
            pltpu.with_memory_space_constraint(a, pltpu.HBM)
            for a in (
                expert_ids.T, gate_weights.T, tokens, gate_proj[0], up_proj[0], down_proj[0]
            )
        )
    )


def solution(mesh):
    placed = (
        P("expert", "dp"),
        P("expert", None),
        P("expert", None),
        P("expert", "dp", None),
        P("expert", "dp", None),
        P("expert", None, "dp"),
    )
    return jax.shard_map(
        body, mesh=mesh, in_specs=placed, out_specs=P("expert", "dp"), check_vma=False
    )
```
